128 devices in a mesh: rows: 16 (over z, x), sub: 8 (over y, core).
Axes of the slice: x: 4, y: 4, z: 4, core: 2. Of those that a mesh axis runs over, the one named last changes fastest.
Arguments:
- residuals: bfloat16 [65536, 1024], P(('rows', 'sub')), may hold values from -14 to 14
- codes: int32 [65536, 64], P(('rows', 'sub')), may hold values from 0 to 255, as said below
- codebook: bfloat16 [64, 16, 256], replicated, may hold values from -4 to 4
Outputs:
- rotated: bfloat16 [65536, 1024], P(('rows', 'sub'))
- new_codebook: float32 [64, 16, 256], P('sub', None, 'rows')
The draws below stay inside these ranges and needn't reach their ends.
Inputs may be any that keep to these rules, and one draw needn't show every extreme that they name: `codes`: every codeword 0 to 255 occurs in every column.
All inputs are finite; a program needn't handle non-finite values.
Results may differ from the reference program's by a relative error of at most 0.0042.
Values may be sent and summed in bfloat16 or wider, within the bound.
A program may use at most 64 MiB of HBM per device.

```python
import jax
import jax.numpy as jnp
from jax import lax

D = 1024
SUBS = 64
CODES = 256
ITERS = 2
SUBDIM = 16
ROWS = 65536


def make_codes(key):
    base = jax.random.fold_in(key, 11)
    table = jax.random.randint(base, (ROWS, SUBS), 0, CODES)
    shifts = jax.random.randint(jax.random.fold_in(base, 1), (1, SUBS), 0, CODES)
    first = (jnp.arange(CODES, dtype=jnp.int32)[:, None] + shifts) % CODES
    return table.at[:CODES].set(first.astype(table.dtype))


def make_book(key):
    values = jax.random.normal(jax.random.fold_in(key, 22), (SUBS, SUBDIM, CODES), jnp.float32)
    return jnp.clip(values, -4.0, 4.0)


def draw_codes(key, part):
    return make_codes(key).astype(jnp.int32)


def draw_codebook(key, part):
    return make_book(key).astype(jnp.bfloat16)


def draw_residuals(key, part):
    labels = make_codes(key)
    book = jnp.transpose(make_book(key), (0, 2, 1))
    recon = book[jnp.arange(SUBS)[None, :], labels].reshape(ROWS, D)
    order = jax.random.permutation(jax.random.fold_in(key, 33), D)
    along = jnp.arange(ROWS, dtype=jnp.float32) / ROWS
    jitter = jax.random.uniform(jax.random.fold_in(key, 44), (ROWS,), jnp.float32, 0.5, 1.5)
    mixing = (0.1 + 2.0 * along * along * along) * jitter
    noise = jnp.clip(jax.random.normal(jax.random.fold_in(key, 55), (ROWS, D), jnp.float32), -4.0, 4.0)
    offset = jnp.clip(jax.random.normal(jax.random.fold_in(key, 66), (D,), jnp.float32), -2.0, 2.0)
    drift = 1.5 * (2.0 * along - 1.0)
    values = recon + mixing[:, None] * recon[:, order] + 0.5 * noise + drift[:, None] * offset[None, :]
    return jnp.clip(values, -14.0, 14.0).astype(jnp.bfloat16)


def setup_inputs(seed: int = 0) -> dict:
    streams_of = jax.random.split(jax.random.key(seed), 4)
    residuals = draw_residuals(jax.random.fold_in(streams_of[3], 71), 0)
    codes = draw_codes(jax.random.fold_in(streams_of[3], 71), 0)
    codebook = draw_codebook(jax.random.fold_in(streams_of[3], 71), 0)
    return {"residuals": residuals, "codes": codes, "codebook": codebook}


def lookup(codes_blk, book):
    levels = jnp.arange(CODES, dtype=jnp.int32)
    hot = (codes_blk[:, :, None] == levels[None, None, :]).astype(jnp.float32)
    rec = jnp.einsum('rmk,mdk->rmd', hot, book.astype(jnp.float32))
    return rec.reshape(codes_blk.shape[0], D).astype(jnp.bfloat16)

def reference(residuals, codes, codebook):
    blocks = ROWS // 512
    recon = lax.map(lambda c: lookup(c, codebook), codes.reshape(blocks, 512, SUBS)).reshape(ROWS, D)
    cross = lax.dot_general(residuals, recon, (((0,), (0,)), ((), ())), preferred_element_type=jnp.float32)
    highest = lax.Precision.HIGHEST
    contract = (((0,), (0,)), ((), ()))
    polar = cross / jnp.sqrt(jnp.sum(cross * cross) + 1e-06)
    gram = lax.dot_general(polar, polar, contract, precision=highest)
    scale = jnp.sqrt(jnp.sqrt(jnp.sum(gram * gram) + 1e-06))
    polar = polar / scale
    gram = gram / (scale * scale)
    for step in range(ITERS):
        if step > 0:
            gram = lax.dot_general(polar, polar, contract, precision=highest)
        moved = jnp.dot(polar, gram, precision=highest)
        polar = 3.4445 * polar - 4.775 * moved + 2.0315 * jnp.dot(moved, gram, precision=highest)
    rotation = polar.astype(jnp.bfloat16)
    rotated = jnp.dot(residuals, rotation, preferred_element_type=jnp.float32).astype(jnp.bfloat16)
    levels = jnp.arange(CODES, dtype=jnp.int32)

    def accumulate(carry, piece):
        sums, counts = carry
        values, labels = piece
        hot = (labels[:, :, None] == levels[None, None, :]).astype(jnp.float32)
        sums = sums + jnp.einsum('rmd,rmk->mdk', values.reshape(512, SUBS, SUBDIM).astype(jnp.float32), hot)
        counts = counts + lax.optimization_barrier(jnp.sum(hot, axis=0))
        return ((sums, counts), None)
    start = (jnp.zeros((SUBS, SUBDIM, CODES), jnp.float32), jnp.zeros((SUBS, CODES), jnp.float32))
    (sums, counts), unused = lax.scan(accumulate, start, (rotated.reshape(blocks, 512, D), codes.reshape(blocks, 512, SUBS)))
    return (rotated, sums / counts[:, None, :])
```

```python
import jax
import jax.numpy as jnp
from jax import lax
from jax.experimental import pallas as pl
from jax.experimental.pallas import tpu as pltpu
from jax.sharding import PartitionSpec as P

D = 1024
SUBS = 64
CODES = 256
SUBDIM = 16
LANES = 128
A, B, C = 3.4445, -4.775, 2.0315
MESH = pl.DeviceIdType.MESH
F32 = jnp.float32
BF16 = jnp.bfloat16
COLS = ((0, 384), (384, 384), (768, 256))
ORDERS = (("z", "x", "y"), ("x", "y", "z"), ("y", "z", "x"))
NT = (((1,), (1,)), ((), ()))


class Here:
    def __init__(self):
        rows, sub = lax.axis_index("rows"), lax.axis_index("sub")
        self.at = {"z": rows // 4, "x": rows % 4, "y": sub // 2, "c": sub % 2}

    def device(self, axis, value):
        at = dict(self.at)
        at[axis] = value
        return (at["z"] * 4 + at["x"], at["y"] * 2 + at["c"])

    def peers(self, axis):
        size = 2 if axis == "c" else 4
        me = self.at[axis]
        return [(j - 1, (me + j) % size) for j in range(1, size)]

    def greet(self):
        barrier = pltpu.get_barrier_semaphore()
        for axis in "czxy":
            for _, other in self.peers(axis):
                pl.semaphore_signal(
                    barrier, inc=1, device_id=self.device(axis, other), device_id_type=MESH
                )
        pl.semaphore_wait(barrier, 10)

    def send(self, src, dst, send_sem, recv_sem, axis, other):
        copy = pltpu.make_async_remote_copy(
            src_ref=src,
            dst_ref=dst,
            send_sem=send_sem,
            recv_sem=recv_sem,
            device_id=self.device(axis, other),
            device_id_type=MESH,
        )
        copy.start()
        return copy


def hot_of(labels_ref, m, levels):
    row = labels_ref[pl.ds(m, 1), :]
    return jnp.where(levels == row, 1.0, 0.0).astype(BF16)


def rows_of(start, size):
    return pl.ds(pl.multiple_of(start, size), size)


def cross_kernel(labels_ref, book_ref, x_ref, out_ref, recon, part, got0, got1, got2, got3, ssem, rsem):
    here = Here()
    rows = x_ref.shape[0]
    levels = lax.broadcasted_iota(jnp.int32, (CODES, rows), 0)

    def one(m, carry):
        hot = hot_of(labels_ref, m, levels)
        rec = jnp.dot(book_ref[m], hot, preferred_element_type=F32)
        recon[rows_of(m * SUBDIM, SUBDIM), :] = rec.astype(BF16)
        return carry

    lax.fori_loop(0, SUBS, one, 0, unroll=4)
    here.greet()
    core = here.at["c"]
    mine, theirs = rows_of(core * 512, 512), rows_of((1 - core) * 512, 512)
    pending = []
    flight = {}
    for t, (first, width) in enumerate(COLS):
        cols = pl.ds(first, width)
        part[:, cols] = jnp.dot(recon[...], x_ref[:, cols], preferred_element_type=F32)
        flight[t] = here.send(
            part.at[theirs, cols], got0.at[:, cols], ssem.at[t, 0, 0], rsem.at[t, 0, 0], "c", 1 - core
        )
    base = {}
    for t, (first, width) in enumerate(COLS):
        cols = pl.ds(first, width)
        flight[t].wait_recv()
        pending.append(flight[t])
        part[mine, cols] += got0[:, cols]
        base[t] = core * 512
    size = 512
    for k, got in enumerate((got1, got2, got3)):
        size = size // 4
        for t, (first, width) in enumerate(COLS):
            cols = pl.ds(first, width)
            axis = ORDERS[t][k]
            flight[t] = []
            for slot, other in here.peers(axis):
                flight[t].append(
                    here.send(
                        part.at[rows_of(base[t] + other * size, size), cols],
                        got.at[slot, :, cols],
                        ssem.at[t, k + 1, slot],
                        rsem.at[t, k + 1, slot],
                        axis,
                        other,
                    )
                )
        for t, (first, width) in enumerate(COLS):
            cols = pl.ds(first, width)
            base[t] = base[t] + here.at[ORDERS[t][k]] * size
            for copy in flight[t]:
                copy.wait_recv()
                pending.append(copy)
            block = rows_of(base[t], size)
            total = (part[block, cols] + got[0, :, cols]) + (got[1, :, cols] + got[2, :, cols])
            if k < 2:
                part[block, cols] = total
            else:
                out_ref[block, cols] = total
    for k in (2, 1, 0):
        for t, (first, width) in enumerate(COLS):
            cols = pl.ds(first, width)
            axis = ORDERS[t][k]
            flight[t] = []
            block = rows_of(base[t], size)
            for slot, other in here.peers(axis):
                flight[t].append(
                    here.send(
                        out_ref.at[block, cols],
                        out_ref.at[block, cols],
                        ssem.at[t, 4 + k, slot],
                        rsem.at[t, 4 + k, slot],
                        axis,
                        other,
                    )
                )
        for t in range(3):
            for copy in flight[t]:
                copy.wait_recv()
                pending.append(copy)
            base[t] = base[t] - here.at[ORDERS[t][k]] * size
        size = size * 4
    for t, (first, width) in enumerate(COLS):
        cols = pl.ds(first, width)
        flight[t] = here.send(
            out_ref.at[mine, cols], out_ref.at[mine, cols], ssem.at[t, 7, 0], rsem.at[t, 7, 0], "c", 1 - core
        )
    for t in range(3):
        flight[t].wait_recv()
        pending.append(flight[t])
    for copy in pending:
        copy.wait_send()


def reduced_cross(labels, codebook, residuals):
    rows = residuals.shape[0]
    vmem = pl.BlockSpec(memory_space=pltpu.VMEM)
    return pl.pallas_call(
        cross_kernel,
        out_shape=jax.ShapeDtypeStruct((D, D), F32),
        in_specs=[vmem] * 3,
        out_specs=vmem,
        scratch_shapes=[
            pltpu.VMEM((D, rows), BF16),
            pltpu.VMEM((D, D), F32),
            pltpu.VMEM((512, D), F32),
            pltpu.VMEM((3, 128, D), F32),
            pltpu.VMEM((3, 32, D), F32),
            pltpu.VMEM((3, 8, D), F32),
            pltpu.SemaphoreType.DMA((3, 8, 3)),
            pltpu.SemaphoreType.DMA((3, 8, 3)),
        ],
        compiler_params=pltpu.CompilerParams(
            collective_id=0, has_side_effects=True, vmem_limit_bytes=48 * 2**20
        ),
    )(labels, codebook, residuals)


def split(value):
    high = value.astype(BF16)
    return high, (value - high.astype(F32)).astype(BF16)


def dot3(ah, al, bh, bl, dims):
    def dot(a, b):
        return lax.dot_general(a, b, dims, preferred_element_type=F32)

    return dot(ah, bh) + (dot(ah, bl) + dot(al, bh))


STEP = 256


def symmetric(out, lh, ll, rh, rl):
    total = jnp.zeros((STEP, STEP), F32)
    for i in range(D // STEP):
        band = slice(i * STEP, (i + 1) * STEP)
        rest = slice(i * STEP, D)
        block = dot3(lh[band, :], ll[band, :], rh[rest, :], rl[rest, :], NT)
        out[band, rest] = block
        for j in range(i + 1, D // STEP):
            piece = block[:, (j - i) * STEP : (j - i + 1) * STEP]
            out[j * STEP : (j + 1) * STEP, band] = piece.T


def squares(ref):
    def one(i, total):
        block = ref[rows_of(i * 64, 64), :]
        return total + jnp.sum((block * block).reshape(8, 8, D), axis=0)

    total = lax.fori_loop(0, D // 64, one, jnp.zeros((8, D), F32))
    return jnp.sum(jnp.sum(total, axis=1, keepdims=True), axis=0, keepdims=True)


def iterate_kernel(cross_ref, labels_ref, x_ref, rot_ref, sums_ref, counts_ref, ah, al, gh, gl, gram, square):
    NN = (((1,), (0,)), ((), ()))
    norm = 1.0 / jnp.sqrt(squares(cross_ref) + 1e-06)

    def load(i, carry):
        band = rows_of(i * 64, 64)
        ah[band, :], al[band, :] = split(cross_ref[band, :] * norm)
        return carry

    lax.fori_loop(0, D // 64, load, 0)

    def split_gram(i, carry):
        band = rows_of(i * 64, 64)
        gh[band, :], gl[band, :] = split(gram[band, :])
        return carry

    for step in range(2):
        symmetric(gram, ah, al, ah, al)
        lax.fori_loop(0, D // 64, split_gram, 0)
        if step == 0:
            scale = jnp.sqrt(jnp.sqrt(squares(gram) + 1e-06))
            back = 1.0 / scale
        else:
            back = jnp.ones((1, 1), F32)
        ca, cb, cc = A * back, B * (back * back * back), C * (back * back * back * back * back)
        symmetric(square, gh, gl, gh, gl)

        def mix(i, carry):
            band = rows_of(i * 64, 64)
            row = lax.broadcasted_iota(jnp.int32, (64, D), 0) + i * 64
            col = lax.broadcasted_iota(jnp.int32, (64, D), 1)
            value = cb * gram[band, :] + cc * square[band, :]
            value = value + jnp.where(row == col, ca, 0.0)
            gh[band, :], gl[band, :] = split(value)
            return carry

        lax.fori_loop(0, D // 64, mix, 0)

        def move(i, carry):
            band = rows_of(i * STEP, STEP)
            square[band, :] = dot3(gh[band, :], gl[band, :], ah[...], al[...], NN)
            return carry

        lax.fori_loop(0, D // STEP, move, 0)

        def keep(i, carry):
            band = rows_of(i * 64, 64)
            ah[band, :], al[band, :] = split(square[band, :])
            return carry

        lax.fori_loop(0, D // 64, keep, 0)

    rows = x_ref.shape[0]
    rot_ref[...] = lax.dot_general(x_ref[...], ah[...], NT, preferred_element_type=F32).astype(BF16)
    levels = lax.broadcasted_iota(jnp.int32, (CODES, rows), 0)
    lane = lax.broadcasted_iota(jnp.int32, (CODES, LANES), 1)
    ones = jnp.ones((rows, LANES), BF16)
    counts_ref[...] = jnp.zeros_like(counts_ref)

    def tally(s, carry):
        cols = pl.ds(pl.multiple_of(s * LANES, LANES), LANES)
        side = jnp.concatenate([rot_ref[:, cols], ones], axis=1)
        sums = jnp.zeros((CODES, LANES), F32)
        counts = counts_ref[...]
        for mm in range(8):
            m = s * 8 + mm
            both = jnp.dot(hot_of(labels_ref, m, levels), side, preferred_element_type=F32)
            sums = jnp.where(lane // SUBDIM == mm, both[:, :LANES], sums)
            counts = jnp.where(lane == m, both[:, LANES:], counts)
        sums_ref[s] = sums
        counts_ref[...] = counts
        return carry

    lax.fori_loop(0, 8, tally, 0)


def rotate_and_tally(cross, labels, residuals):
    rows = residuals.shape[0]
    vmem = pl.BlockSpec(memory_space=pltpu.VMEM)
    return pl.pallas_call(
        iterate_kernel,
        out_shape=(
            jax.ShapeDtypeStruct((rows, D), BF16),
            jax.ShapeDtypeStruct((8, CODES, LANES), F32),
            jax.ShapeDtypeStruct((CODES, LANES), F32),
        ),
        in_specs=[vmem] * 3,
        out_specs=[vmem] * 3,
        scratch_shapes=[pltpu.VMEM((D, D), BF16)] * 4 + [pltpu.VMEM((D, D), F32)] * 2,
        compiler_params=pltpu.CompilerParams(vmem_limit_bytes=56 * 2**20),
    )(cross, labels, residuals)


def means_kernel(sums_ref, counts_ref, out_ref, half, g0, gc0, ga, gb, gc1, gc2, gd, ge, gf, ssem, rsem):
    here = Here()
    here.greet()
    z, x, y, core = (here.at[a] for a in "zxyc")
    pending = []
    number = [0]

    def go(src, dst, axis, other):
        n = number[0]
        number[0] += 1
        copy = here.send(src, dst, ssem.at[n], rsem.at[n], axis, other)
        pending.append(copy)
        return copy

    def got(copies):
        for copy in copies:
            copy.wait_recv()

    first = [go(sums_ref.at[:, 1 - core], g0, "c", 1 - core)]
    second = [go(counts_ref, gc0, "c", 1 - core)]
    got(first)
    for i in range(4):
        half[i] = sums_ref[i, core] + g0[i]
    za = [go(half.at[:, o, :, 0], ga.at[n], "z", o) for n, o in here.peers("z")]
    yb = [go(half.at[o, :, :, 1], gb.at[n], "y", o) for n, o in here.peers("y")]
    got(second)
    gc0[...] += counts_ref[...]
    zc = [go(gc0.at[o], gc1.at[n], "z", o) for n, o in here.peers("z")]
    got(za)
    half[:, z, :, 0] = half[:, z, :, 0] + ga[0] + ga[1] + ga[2]
    xa = [go(half.at[:, z, o, 0], gd.at[n], "x", o) for n, o in here.peers("x")]
    got(yb)
    half[y, :, :, 1] = half[y, :, :, 1] + gb[0] + gb[1] + gb[2]
    zb = [go(half.at[y, o, :, 1], ge.at[n], "z", o) for n, o in here.peers("z")]
    got(zc)
    gc0[z] = gc0[z] + gc1[0] + gc1[1] + gc1[2]
    xc = [go(gc0.at[z, o], gc2.at[n], "x", o) for n, o in here.peers("x")]
    got(xa)
    half[:, z, x, 0] = half[:, z, x, 0] + gd[0] + gd[1] + gd[2]
    ya = [go(half.at[o, z, x, 0], gf.at[0, n], "y", o) for n, o in here.peers("y")]
    got(zb)
    half[y, z, :, 1] = half[y, z, :, 1] + ge[0] + ge[1] + ge[2]
    xb = [go(half.at[y, z, o, 1], gf.at[1, n], "x", o) for n, o in here.peers("x")]
    got(xc)
    gc2[3] = gc0[z, x] + gc2[0] + gc2[1] + gc2[2]
    yc = [go(gc2.at[3], gc2.at[4 + n], "y", o) for n, o in here.peers("y")]
    got(ya)
    low = half[y, z, x, 0] + gf[0, 0] + gf[0, 1] + gf[0, 2]
    got(xb)
    high = half[y, z, x, 1] + gf[1, 0] + gf[1, 1] + gf[1, 2]
    got(yc)
    count = gc2[3] + gc2[4] + gc2[5] + gc2[6]
    row = lax.broadcasted_iota(jnp.int32, (LANES, LANES), 0)
    col = lax.broadcasted_iota(jnp.int32, (LANES, LANES), 1)
    spread = jnp.where(row == (y * 2 + core) * 8 + col // SUBDIM, 1.0, 0.0)
    count = jnp.dot(count, spread, precision=lax.Precision.HIGHEST, preferred_element_type=F32)
    mean = jnp.concatenate([low, high], axis=0) / count
    out_ref[...] = mean.T
    for copy in pending:
        copy.wait_send()


def means(sums, counts):
    vmem = pl.BlockSpec(memory_space=pltpu.VMEM)
    tile = (8, LANES)
    return pl.pallas_call(
        means_kernel,
        out_shape=jax.ShapeDtypeStruct((LANES, 16), F32),
        in_specs=[vmem] * 2,
        out_specs=vmem,
        scratch_shapes=[
            pltpu.VMEM((4, 4, 4, 2) + tile, F32),
            pltpu.VMEM((4, 4, 4, 2) + tile, F32),
            pltpu.VMEM((4, 4, 16, LANES), F32),
            pltpu.VMEM((3, 4, 4) + tile, F32),
            pltpu.VMEM((3, 4, 4) + tile, F32),
            pltpu.VMEM((3, 4, 16, LANES), F32),
            pltpu.VMEM((7, 16, LANES), F32),
            pltpu.VMEM((3, 4) + tile, F32),
            pltpu.VMEM((3, 4) + tile, F32),
            pltpu.VMEM((2, 3) + tile, F32),
            pltpu.SemaphoreType.DMA((32,)),
            pltpu.SemaphoreType.DMA((32,)),
        ],
        compiler_params=pltpu.CompilerParams(
            collective_id=1, has_side_effects=True, vmem_limit_bytes=32 * 2**20
        ),
    )(sums.reshape((4, 2, 4, 4, 2) + tile), counts.reshape(4, 4, 16, LANES))


def per_device(residuals, codes, codebook):
    labels = codes.T
    cross = reduced_cross(labels, codebook, residuals)
    rotated, sums, counts = rotate_and_tally(cross, labels, residuals)
    return rotated, means(sums, counts).reshape(8, SUBDIM, 16)


def solution(mesh):
    return jax.shard_map(
        per_device,
        mesh=mesh,
        in_specs=(P(("rows", "sub"), None), P(("rows", "sub"), None), P()),
        out_specs=(P(("rows", "sub"), None), P("sub", None, "rows")),
        check_vma=False,
    )
```

```python
import jax
import jax.numpy as jnp
from jax import lax
from jax.experimental import pallas as pl
from jax.experimental.pallas import tpu as pltpu
from jax.sharding import PartitionSpec as P

D = 1024
SUBS = 64
CODES = 256
SUBDIM = 16
LANES = 128
A, B, C = 3.4445, -4.775, 2.0315
MESH = pl.DeviceIdType.MESH
F32 = jnp.float32
BF16 = jnp.bfloat16
NN = (((1,), (0,)), ((), ()))
NT = (((1,), (1,)), ((), ()))
STEP = 256
BANDS = D // STEP
CHUNKS = (
    (0, 256, "z", "xy"),
    (256, 256, "x", "yz"),
    (512, 256, "y", "zx"),
    (768, 128, "z", "xy"),
    (896, 128, "x", "yz"),
)
EARLY, LATE = (0, 1, 2), (3, 4)
SPLIT = 768


class Here:
    def __init__(self, ssem, rsem):
        rows, sub = lax.axis_index("rows"), lax.axis_index("sub")
        self.at = {"z": rows // 4, "x": rows % 4, "y": sub // 2, "c": sub % 2}
        self.ssem, self.rsem, self.used = ssem, rsem, 0
        self.pending = []

    def device(self, **where):
        at = {**self.at, **where}
        return (at["z"] * 4 + at["x"], at["y"] * 2 + at["c"])

    def off(self, axis, by):
        return (self.at[axis] + by) % 4

    def send(self, src, dst, **where):
        copy = pltpu.make_async_remote_copy(
            src_ref=src,
            dst_ref=dst,
            send_sem=self.ssem.at[self.used],
            recv_sem=self.rsem.at[self.used],
            device_id=self.device(**where),
            device_id_type=MESH,
        )
        self.used += 1
        copy.start()
        self.pending.append(copy)
        return copy

    def greet(self):
        barrier = pltpu.get_barrier_semaphore()

        def signal(**where):
            pl.semaphore_signal(
                barrier, inc=1, device_id=self.device(**where), device_id_type=MESH
            )

        signal(c=1 - self.at["c"])
        for n in range(1, 64):
            signal(z=self.off("z", n // 16), x=self.off("x", n // 4 % 4), y=self.off("y", n % 4))

    def meet(self):
        pl.semaphore_wait(pltpu.get_barrier_semaphore(), 64)

    def drain(self):
        for copy in self.pending:
            copy.wait_send()
        self.pending = []


def arrive(copies):
    for copy in copies:
        copy.wait_recv()


def rows_of(start, size):
    return pl.ds(pl.multiple_of(start, size), size)


def dot(a, b, dims=NN):
    return lax.dot_general(a, b, dims, preferred_element_type=F32)


def split(value):
    high = value.astype(BF16)
    return high, (value - high.astype(F32)).astype(BF16)


def total_of(value):
    return jnp.sum(jnp.sum(value, axis=0, keepdims=True), axis=1, keepdims=True)


def diagonal():
    row = lax.broadcasted_iota(jnp.int32, (STEP, STEP), 0)
    return row == lax.broadcasted_iota(jnp.int32, (STEP, STEP), 1)


def upper(i, h, l, depth):
    band, rest = slice(i * STEP, (i + 1) * STEP), slice((i + 1) * STEP, D)
    mixed = dot(l[band, depth], h[band, depth], NT)
    block = dot(h[band, depth], h[band, depth], NT) + (mixed + mixed.T)
    if i == BANDS - 1:
        return block, None
    side = dot(h[band, depth], h[rest, depth], NT)
    side = side + (dot(h[band, depth], l[rest, depth], NT) + dot(l[band, depth], h[rest, depth], NT))
    return block, side


def store_split(h, l, i, block, side):
    band = slice(i * STEP, (i + 1) * STEP)
    h[band, band], l[band, band] = split(block)
    if side is not None:
        rest = slice((i + 1) * STEP, D)
        h[band, rest], l[band, rest] = split(side)
        h[rest, band], l[rest, band] = split(side.T)


def kernel(labels_hbm, book_hbm, x_hbm, rot_hbm, mean_ref, *scratch):
    (labels, book, x, hot, recon, part, full, got0, got1, got2, ah, al, gh, gl, qh, ql, bh, bl, rot) = scratch[:19]
    (slab, pair, sums_in, counts, countz, countx, county, local, ssem, rsem) = scratch[19:]
    here = Here(ssem, rsem)
    copies = [
        pltpu.make_async_copy(src, dst, local.at[n])
        for n, (src, dst) in enumerate(((labels_hbm, labels), (book_hbm, book), (x_hbm, x)))
    ]
    for copy in copies:
        copy.start()
    here.greet()
    z, xx, y, core = (here.at[a] for a in "zxyc")
    rows = x.shape[0]
    copies[0].wait()
    copies[1].wait()
    levels = lax.broadcasted_iota(jnp.int32, (CODES, rows), 0)

    def rebuild(m, carry):
        one = jnp.where(levels == labels[pl.ds(m, 1), :], 1.0, 0.0).astype(BF16)
        hot[m] = one
        recon[rows_of(m * SUBDIM, SUBDIM), :] = dot(book[m], one).astype(BF16)
        return carry

    lax.fori_loop(0, SUBS, rebuild, 0, unroll=8)
    copies[2].wait()
    here.meet()

    mine, theirs = rows_of(core * 512, 512), rows_of((1 - core) * 512, 512)
    flight, base = {}, {}

    def cols_of(t):
        return pl.ds(CHUNKS[t][0], CHUNKS[t][1])

    def stage_core(t):
        cols = cols_of(t)
        flight[t] = [here.send(part.at[theirs, cols], got0.at[:, cols], c=1 - core)]

    def stage_first(t):
        cols, axis = cols_of(t), CHUNKS[t][2]
        arrive(flight[t])
        part[mine, cols] += got0[:, cols]
        flight[t] = []
        for j in range(1, 4):
            other = here.off(axis, j)
            src = part.at[rows_of(core * 512 + other * 128, 128), cols]
            flight[t].append(here.send(src, got1.at[j - 1, :, cols], **{axis: other}))
        base[t] = core * 512 + here.at[axis] * 128

    def stage_second(t):
        cols, (p, q) = cols_of(t), CHUNKS[t][3]
        arrive(flight[t])
        block = rows_of(base[t], 128)
        part[block, cols] = (part[block, cols] + got1[0, :, cols]) + (got1[1, :, cols] + got1[2, :, cols])
        flight[t] = []
        for n in range(1, 16):
            i, j = here.off(p, n // 4), here.off(q, n % 4)
            src = part.at[rows_of(base[t] + (i * 4 + j) * 8, 8), cols]
            flight[t].append(here.send(src, got2.at[n - 1, :, cols], **{p: i, q: j}))

    def stage_back(t):
        cols, (p, q) = cols_of(t), CHUNKS[t][3]
        arrive(flight[t])
        own = rows_of(base[t] + (here.at[p] * 4 + here.at[q]) * 8, 8)
        total = part[own, cols]
        for n in range(15):
            total = total + got2[n, :, cols]
        full[own, cols] = total
        flight[t] = []
        for n in range(1, 16):
            i, j = here.off(p, n // 4), here.off(q, n % 4)
            flight[t].append(here.send(full.at[own, cols], full.at[own, cols], **{p: i, q: j}))

    def stage_wide(t):
        cols, axis = cols_of(t), CHUNKS[t][2]
        arrive(flight[t])
        block = rows_of(base[t], 128)
        flight[t] = []
        for j in range(1, 4):
            other = here.off(axis, j)
            flight[t].append(here.send(full.at[block, cols], full.at[block, cols], **{axis: other}))

    def stage_last(t):
        cols = cols_of(t)
        arrive(flight[t])
        flight[t] = [here.send(full.at[mine, cols], full.at[mine, cols], c=1 - core)]

    for first in range(0, D, STEP):
        cols = pl.ds(first, STEP)
        part[:, cols] = dot(recon[...], x[:, cols])
        for t in range(5):
            if first <= CHUNKS[t][0] < first + STEP:
                stage_core(t)
    for t in EARLY + LATE:
        stage_first(t)

    lane = lax.broadcasted_iota(jnp.int32, (CODES, LANES), 1)
    ones = jnp.ones((rows, LANES), BF16)
    counts[0] = jnp.zeros((CODES, LANES), F32)

    def count(g, carry):
        value = counts[0]
        for mm in range(8):
            m = g * 8 + mm
            value = jnp.where(lane == m, dot(hot[m], ones), value)
        counts[0] = value
        return carry

    lax.fori_loop(0, 8, count, 0)
    count_flight = [here.send(counts.at[0], counts.at[1], c=1 - core)]
    for t in EARLY:
        stage_second(t)
    arrive(count_flight)
    counts[2] = counts[0] + counts[1]
    count_flight = []
    for j in range(1, 4):
        other = here.off("z", j)
        src = counts.at[2, rows_of(other * 64, 64)]
        count_flight.append(here.send(src, countz.at[j - 1], z=other))
    for t in LATE:
        stage_second(t)
    for t in EARLY:
        stage_back(t)
    arrive(count_flight)
    countz[3] = (counts[2, rows_of(z * 64, 64)] + countz[0]) + (countz[1] + countz[2])
    count_flight = []
    for j in range(1, 4):
        other = here.off("x", j)
        count_flight.append(here.send(countz.at[3, rows_of(other * 16, 16)], countx.at[j - 1], x=other))
    for t in LATE:
        stage_back(t)
    for t in EARLY:
        stage_wide(t)
    arrive(count_flight)
    countx[3] = (countz[3, rows_of(xx * 16, 16)] + countx[0]) + (countx[1] + countx[2])
    count_flight = []
    for j in range(1, 4):
        count_flight.append(here.send(countx.at[3], county.at[j - 1], y=here.off("y", j)))
    for t in LATE:
        stage_wide(t)
    for t in EARLY:
        stage_last(t)
    for t in EARLY:
        arrive(flight[t])

    def load(cols):
        def one(i, carry):
            band = rows_of(i * 64, 64)
            ah[band, cols], al[band, cols] = split(full[band, cols])
            return carry

        lax.fori_loop(0, D // 64, one, 0)

    load(slice(0, SPLIT))
    here.drain()
    for t in LATE:
        stage_last(t)
    for i in range(BANDS):
        band, rest = slice(i * STEP, (i + 1) * STEP), slice((i + 1) * STEP, D)
        block, side = upper(i, ah, al, slice(0, SPLIT))
        part[band, band] = block
        if side is not None:
            part[band, rest] = side
    for t in LATE:
        arrive(flight[t])
    load(slice(SPLIT, D))
    trace, square = jnp.zeros((1, 1), F32), jnp.zeros((1, 1), F32)
    for i in range(BANDS):
        band, rest = slice(i * STEP, (i + 1) * STEP), slice((i + 1) * STEP, D)
        block, side = upper(i, ah, al, slice(SPLIT, D))
        block = block + part[band, band]
        trace += total_of(jnp.where(diagonal(), block, 0.0))
        square += total_of(block * block)
        part[band, band] = block
        if side is not None:
            side = side + part[band, rest]
            square += 2.0 * total_of(side * side)
            part[band, rest] = side
        store_split(gh, gl, i, block, side)

    norm = 1.0 / (trace + 1e-06)
    scale = jnp.sqrt(jnp.sqrt(square * norm * norm + 1e-06))
    unit = norm / (scale * scale)
    front = jnp.sqrt(norm) / scale

    def polynomial(front, unit):
        whole = slice(0, D)
        cb, cc = B * front * unit, C * front * unit
        for i in range(BANDS):
            band, rest = slice(i * STEP, (i + 1) * STEP), slice((i + 1) * STEP, D)
            block, side = upper(i, gh, gl, whole)
            block = cb * part[band, band] + cc * (unit * block)
            block = block + jnp.where(diagonal(), A * front, 0.0)
            if side is not None:
                side = cb * part[band, rest] + cc * (unit * side)
            store_split(qh, ql, i, block, side)

    def product(band, h, l):
        return dot(qh[band, :], h[...]) + (dot(qh[band, :], l[...]) + dot(ql[band, :], h[...]))

    polynomial(front, unit)

    def move(i, carry):
        band = rows_of(i * STEP, STEP)
        bh[band, :], bl[band, :] = split(product(band, ah, al))
        return carry

    lax.fori_loop(0, BANDS, move, 0)
    for i in range(BANDS):
        band, rest = slice(i * STEP, (i + 1) * STEP), slice((i + 1) * STEP, D)
        block, side = upper(i, bh, bl, slice(0, D))
        part[band, band] = block
        if side is not None:
            part[band, rest] = side
        store_split(gh, gl, i, block, side)
    one = jnp.ones((1, 1), F32)
    polynomial(one, one)

    outs = []
    for n in range(4):
        to = here.off("y", n + 1)
        band = rows_of(to * STEP, STEP)
        ah[band, :] = product(band, bh, bl).astype(BF16)
        rot[n] = dot(x[...], ah[band, :], NT).astype(BF16)
        outs.append(pltpu.make_async_copy(rot.at[n], rot_hbm.at[:, band], local.at[3 + n]))
        outs[n].start()
        for p in range(2):
            m = (to * 2 + p) * 8
            res = dot(hot[pl.ds(m, 8)].reshape(8 * CODES, rows), rot[n, :, p * LANES : (p + 1) * LANES])
            sums = res[:CODES]
            for mm in range(1, 8):
                sums = jnp.where(lane // SUBDIM == mm, res[mm * CODES : (mm + 1) * CODES], sums)
            slab[n, p] = sums
        swap = here.send(slab.at[n, 1 - core], pair.at[n], c=1 - core)
        swap.wait_recv()
        pair[n] += slab[n, core]
        for k in range(16):
            i, j = here.off("z", k // 4), here.off("x", k % 4)
            block = rows_of((i * 4 + j) * 16, 16)
            if n == 3 and k == 0:
                sums_in[n * 16 + k] = pair[n, block]
            else:
                flight[n, k] = here.send(pair.at[n, block], sums_in.at[n * 16 + k], z=i, x=j, y=to)
    arrive(count_flight)
    count = (countx[3] + county[0]) + (county[1] + county[2])
    row = lax.broadcasted_iota(jnp.int32, (LANES, LANES), 0)
    col = lax.broadcasted_iota(jnp.int32, (LANES, LANES), 1)
    spread = jnp.where(row == (y * 2 + core) * 8 + col // SUBDIM, 1.0, 0.0)
    count = jnp.dot(count, spread, precision=lax.Precision.HIGHEST, preferred_element_type=F32)
    sums = jnp.zeros((16, LANES), F32)
    for n in range(4):
        for k in range(16):
            if (n, k) != (3, 0):
                flight[n, k].wait_recv()
            sums = sums + sums_in[n * 16 + k]
    mean_ref[...] = (sums / count).T
    for copy in outs:
        copy.wait()
    here.drain()


def per_device(residuals, codes, codebook):
    rows = residuals.shape[0]
    anywhere = pl.BlockSpec(memory_space=pl.ANY)
    vmem = pltpu.VMEM
    matrix = [vmem((D, D), BF16)]
    rotated, mean = pl.pallas_call(
        kernel,
        out_shape=(
            jax.ShapeDtypeStruct((rows, D), BF16),
            jax.ShapeDtypeStruct((LANES, 16), F32),
        ),
        in_specs=[anywhere] * 3,
        out_specs=(anywhere, pl.BlockSpec(memory_space=pltpu.VMEM)),
        scratch_shapes=[
            vmem((SUBS, rows), jnp.int32),
            vmem((SUBS, SUBDIM, CODES), BF16),
            vmem((rows, D), BF16),
            vmem((SUBS, CODES, rows), BF16),
            vmem((D, rows), BF16),
            vmem((D, D), F32),
            vmem((D, D), F32),
            vmem((512, D), F32),
            vmem((3, 128, D), F32),
            vmem((15, 8, D), F32),
        ]
        + matrix * 8
        + [
            vmem((4, rows, STEP), BF16),
            vmem((4, 2, CODES, LANES), F32),
            vmem((4, CODES, LANES), F32),
            vmem((64, 16, LANES), F32),
            vmem((3, CODES, LANES), F32),
            vmem((4, 64, LANES), F32),
            vmem((4, 16, LANES), F32),
            vmem((3, 16, LANES), F32),
            pltpu.SemaphoreType.DMA((7,)),
            pltpu.SemaphoreType.DMA((272,)),
            pltpu.SemaphoreType.DMA((272,)),
        ],
        compiler_params=pltpu.CompilerParams(
            collective_id=0, has_side_effects=True, vmem_limit_bytes=62 * 2**20
        ),
    )(codes.T, codebook, residuals)
    return rotated, mean.reshape(8, SUBDIM, 16)


def solution(mesh):
    return jax.shard_map(
        per_device,
        mesh=mesh,
        in_specs=(P(("rows", "sub"), None), P(("rows", "sub"), None), P()),
        out_specs=(P(("rows", "sub"), None), P("sub", None, "rows")),
        check_vma=False,
    )
```

```python
import jax
import jax.numpy as jnp
from jax import lax
from jax.experimental import pallas as pl
from jax.experimental.pallas import tpu as pltpu
from jax.sharding import PartitionSpec as P

D = 1024
SUBS = 64
CODES = 256
SUBDIM = 16
LANES = 128
A, B, C = 3.4445, -4.775, 2.0315
MESH = pl.DeviceIdType.MESH
F32 = jnp.float32
BF16 = jnp.bfloat16
NN = (((1,), (0,)), ((), ()))
NT = (((1,), (1,)), ((), ()))
STEP = 256
BANDS = D // STEP
CHUNKS = (
    (0, 128, "z", "xy"),
    (128, 128, "x", "yz"),
    (256, 128, "y", "zx"),
    (384, 128, "z", "xy"),
    (512, 128, "x", "yz"),
    (640, 128, "y", "zx"),
    (768, 128, "z", "xy"),
    (896, 128, "x", "yz"),
)
GROUPS = ((0, 1, 2), (3, 4, 5), (6, 7))
SPLIT = 768


class Here:
    def __init__(self, ssem, rsem):
        rows, sub = lax.axis_index("rows"), lax.axis_index("sub")
        self.at = {"z": rows // 4, "x": rows % 4, "y": sub // 2, "c": sub % 2}
        self.ssem, self.rsem, self.used = ssem, rsem, 0
        self.pending = []

    def device(self, **where):
        at = {**self.at, **where}
        return (at["z"] * 4 + at["x"], at["y"] * 2 + at["c"])

    def off(self, axis, by):
        return (self.at[axis] + by) % 4

    def send(self, src, dst, **where):
        copy = pltpu.make_async_remote_copy(
            src_ref=src,
            dst_ref=dst,
            send_sem=self.ssem.at[self.used],
            recv_sem=self.rsem.at[self.used],
            device_id=self.device(**where),
            device_id_type=MESH,
        )
        self.used += 1
        copy.start()
        self.pending.append(copy)
        return copy

    def greet(self):
        barrier = pltpu.get_barrier_semaphore()

        def signal(**where):
            pl.semaphore_signal(
                barrier, inc=1, device_id=self.device(**where), device_id_type=MESH
            )

        signal(c=1 - self.at["c"])
        for axis in "zxy":
            for j in range(1, 4):
                signal(**{axis: self.off(axis, j)})

    def meet(self):
        pl.semaphore_wait(pltpu.get_barrier_semaphore(), 10)

    def drain(self, some=None):
        done = list(self.pending) if some is None else some
        for copy in done:
            copy.wait_send()
        self.pending = [copy for copy in self.pending if all(copy is not other for other in done)]


def arrive(copies):
    for copy in copies:
        copy.wait_recv()


def rows_of(start, size):
    return pl.ds(pl.multiple_of(start, size), size)


def dot(a, b, dims=NN):
    return lax.dot_general(a, b, dims, preferred_element_type=F32)


def split(value):
    high = value.astype(BF16)
    return high, (value - high.astype(F32)).astype(BF16)


def total_of(value):
    return jnp.sum(jnp.sum(value, axis=0, keepdims=True), axis=1, keepdims=True)


def diagonal():
    row = lax.broadcasted_iota(jnp.int32, (STEP, STEP), 0)
    return row == lax.broadcasted_iota(jnp.int32, (STEP, STEP), 1)


def corner(i, h, l, depth=slice(0, D)):
    band = slice(i * STEP, (i + 1) * STEP)
    mixed = dot(l[band, depth], h[band, depth], NT)
    return dot(h[band, depth], h[band, depth], NT) + (mixed + mixed.T)


def beside(i, rest, h, l, depth=slice(0, D)):
    band = slice(i * STEP, (i + 1) * STEP)
    side = dot(h[band, depth], h[rest, depth], NT)
    return side + (dot(h[band, depth], l[rest, depth], NT) + dot(l[band, depth], h[rest, depth], NT))


def tiles(*bands):
    for i in bands:
        band, rest = slice(i * STEP, (i + 1) * STEP), slice((i + 1) * STEP, D)
        yield i, band, band
        if i < BANDS - 1:
            yield i, band, rest


def tile(i, band, cols, h, l, depth=slice(0, D)):
    return corner(i, h, l, depth) if band == cols else beside(i, cols, h, l, depth)


def store_split(h, l, band, cols, value):
    h[band, cols], l[band, cols] = split(value)
    if band != cols:
        h[cols, band], l[cols, band] = split(value.T)


def kernel(labels_hbm, book_hbm, x_hbm, rot_ref, mean_ref, *scratch):
    (labels, book, x, hot, recon, part, full, got0, got1, got2, ah, al, gh, gl, qh, ql, bh, bl) = scratch[:18]
    (slab, pair, sums_in, counts, countz, countx, county, local, ssem, rsem) = scratch[18:]
    here = Here(ssem, rsem)
    copies = [
        pltpu.make_async_copy(src, dst, local.at[n])
        for n, (src, dst) in enumerate(((labels_hbm, labels), (book_hbm, book), (x_hbm, x)))
    ]
    for copy in copies:
        copy.start()
    here.greet()
    z, xx, y, core = (here.at[a] for a in "zxyc")
    rows = x.shape[0]
    copies[0].wait()
    copies[1].wait()
    levels = lax.broadcasted_iota(jnp.int32, (CODES, rows), 0)

    def rebuild(m, carry):
        one = jnp.where(levels == labels[pl.ds(m, 1), :], 1.0, 0.0).astype(BF16)
        hot[m] = one
        recon[rows_of(m * SUBDIM, SUBDIM), :] = dot(book[m], one).astype(BF16)
        return carry

    lax.fori_loop(0, SUBS, rebuild, 0, unroll=8)
    copies[2].wait()
    here.meet()

    mine, theirs = rows_of(core * 512, 512), rows_of((1 - core) * 512, 512)
    flight, base = {}, {}

    def cols_of(t):
        return pl.ds(CHUNKS[t][0], CHUNKS[t][1])

    def stage_core(t):
        cols = cols_of(t)
        flight[t] = [here.send(part.at[theirs, cols], got0.at[:, cols], c=1 - core)]

    def stage_first(t):
        cols, axis = cols_of(t), CHUNKS[t][2]
        arrive(flight[t])
        part[mine, cols] += got0[:, cols]
        flight[t] = []
        for j in range(1, 4):
            other = here.off(axis, j)
            src = part.at[rows_of(core * 512 + other * 128, 128), cols]
            flight[t].append(here.send(src, got1.at[j - 1, :, cols], **{axis: other}))
        base[t] = core * 512 + here.at[axis] * 128

    def stage_second(t):
        cols, (p, q) = cols_of(t), CHUNKS[t][3]
        arrive(flight[t])
        block = rows_of(base[t], 128)
        part[block, cols] = (part[block, cols] + got1[0, :, cols]) + (got1[1, :, cols] + got1[2, :, cols])
        flight[t] = []
        for n in range(1, 16):
            i, j = here.off(p, n // 4), here.off(q, n % 4)
            src = part.at[rows_of(base[t] + (i * 4 + j) * 8, 8), cols]
            flight[t].append(here.send(src, got2.at[n - 1, :, cols], **{p: i, q: j}))

    def stage_back(t):
        cols, (p, q) = cols_of(t), CHUNKS[t][3]
        arrive(flight[t])
        own = rows_of(base[t] + (here.at[p] * 4 + here.at[q]) * 8, 8)
        total = part[own, cols]
        for n in range(15):
            total = total + got2[n, :, cols]
        full[own, cols] = total
        flight[t] = []
        for n in range(1, 16):
            i, j = here.off(p, n // 4), here.off(q, n % 4)
            flight[t].append(here.send(full.at[own, cols], full.at[own, cols], **{p: i, q: j}))

    def stage_wide(t):
        cols, axis = cols_of(t), CHUNKS[t][2]
        arrive(flight[t])
        block = rows_of(base[t], 128)
        flight[t] = []
        for j in range(1, 4):
            other = here.off(axis, j)
            flight[t].append(here.send(full.at[block, cols], full.at[block, cols], **{axis: other}))

    def stage_last(t):
        cols = cols_of(t)
        arrive(flight[t])
        flight[t] = [here.send(full.at[mine, cols], full.at[mine, cols], c=1 - core)]

    for first in range(0, D, STEP):
        cols = pl.ds(first, STEP)
        part[:, cols] = dot(recon[...], x[:, cols])
        for t in range(len(CHUNKS)):
            if first <= CHUNKS[t][0] < first + STEP:
                stage_core(t)
    for t in range(len(CHUNKS)):
        stage_first(t)

    lane = lax.broadcasted_iota(jnp.int32, (CODES, LANES), 1)
    ones = jnp.ones((rows, LANES), BF16)
    counts[0] = jnp.zeros((CODES, LANES), F32)

    def count(g, carry):
        value = counts[0]
        for mm in range(8):
            m = g * 8 + mm
            value = jnp.where(lane == m, dot(hot[m], ones), value)
        counts[0] = value
        return carry

    lax.fori_loop(0, 8, count, 0)
    count_flight = [here.send(counts.at[0], counts.at[1], c=1 - core)]
    def go(stage, g):
        for t in GROUPS[g]:
            stage(t)

    for t in GROUPS[0]:
        arrive(flight[t])
        flight[t] = []
    go(stage_second, 0)
    arrive(count_flight)
    counts[2] = counts[0] + counts[1]
    count_flight = []
    for j in range(1, 4):
        other = here.off("z", j)
        src = counts.at[2, rows_of(other * 64, 64)]
        count_flight.append(here.send(src, countz.at[j - 1], z=other))
    go(stage_second, 1)
    go(stage_back, 0)
    arrive(count_flight)
    countz[3] = (counts[2, rows_of(z * 64, 64)] + countz[0]) + (countz[1] + countz[2])
    count_flight = []
    for j in range(1, 4):
        other = here.off("x", j)
        count_flight.append(here.send(countz.at[3, rows_of(other * 16, 16)], countx.at[j - 1], x=other))
    go(stage_second, 2)
    reads_part = list(here.pending)
    go(stage_back, 1)
    go(stage_wide, 0)
    arrive(count_flight)
    countx[3] = (countz[3, rows_of(xx * 16, 16)] + countx[0]) + (countx[1] + countx[2])
    count_flight = []
    for j in range(1, 4):
        count_flight.append(here.send(countx.at[3], county.at[j - 1], y=here.off("y", j)))
    go(stage_back, 2)
    go(stage_wide, 1)
    go(stage_wide, 2)
    go(stage_last, 0)
    go(stage_last, 1)
    for t in GROUPS[0] + GROUPS[1]:
        arrive(flight[t])

    def load(cols):
        def one(i, carry):
            band = rows_of(i * 64, 64)
            ah[band, cols], al[band, cols] = split(full[rows_of((i * 64 + core * 512) % D, 64), cols])
            return carry

        lax.fori_loop(0, D // 64, one, 0)

    load(slice(0, SPLIT))
    here.drain(reads_part)
    go(stage_last, 2)
    for i, band, cols in tiles(0, 1, 2, 3):
        part[band, cols] = tile(i, band, cols, ah, al, slice(0, SPLIT))
    for t in GROUPS[2]:
        arrive(flight[t])
    load(slice(SPLIT, D))
    trace, square = jnp.zeros((1, 1), F32), jnp.zeros((1, 1), F32)
    for i, band, cols in tiles(0, 1, 2, 3):
        value = tile(i, band, cols, ah, al, slice(SPLIT, D)) + part[band, cols]
        if band == cols:
            trace += total_of(jnp.where(diagonal(), value, 0.0))
            square += total_of(value * value)
        else:
            square += 2.0 * total_of(value * value)
        part[band, cols] = value
        store_split(gh, gl, band, cols, value)

    norm = 1.0 / (trace + 1e-06)
    scale = jnp.sqrt(jnp.sqrt(square * norm * norm + 1e-06))
    unit = norm / (scale * scale)
    front = jnp.sqrt(norm) / scale

    def polynomial(front, unit):
        cb, cc = B * front * unit, C * front * unit
        for i, band, cols in tiles(0, 1, 2, 3):
            value = cb * part[band, cols] + cc * (unit * tile(i, band, cols, gh, gl))
            if band == cols:
                value = value + jnp.where(diagonal(), A * front, 0.0)
            store_split(qh, ql, band, cols, value)

    def product(band, h, l):
        return dot(qh[band, :], h[...]) + (dot(qh[band, :], l[...]) + dot(ql[band, :], h[...]))

    polynomial(front, unit)

    halves = []
    for i in range(2):
        band, there = slice(i * STEP, (i + 1) * STEP), slice(512 + i * STEP, 512 + (i + 1) * STEP)
        bh[band, :], bl[band, :] = split(product(band, ah, al))
        halves.append(here.send(bh.at[band], bh.at[there], c=1 - core))
        halves.append(here.send(bl.at[band], bl.at[there], c=1 - core))

    def gram(i, band, cols):
        value = tile(i, band, cols, bh, bl)
        part[band, cols] = value
        store_split(gh, gl, band, cols, value)

    low, high, right = slice(0, STEP), slice(STEP, 512), slice(512, D)
    gram(0, low, low)
    gram(0, low, high)
    gram(1, high, high)
    arrive(halves)
    gram(0, low, right)
    gram(1, high, right)
    for i, band, cols in tiles(2, 3):
        gram(i, band, cols)
    one = jnp.ones((1, 1), F32)
    polynomial(one, one)

    arrive(count_flight)
    count = (countx[3] + county[0]) + (county[1] + county[2])
    row = lax.broadcasted_iota(jnp.int32, (LANES, LANES), 0)
    col = lax.broadcasted_iota(jnp.int32, (LANES, LANES), 1)
    spread = jnp.where(row == (y * 2 + core) * 8 + col // SUBDIM, 1.0, 0.0)
    count = jnp.dot(count, spread, precision=lax.Precision.HIGHEST, preferred_element_type=F32)

    turned = {}

    def turn(n):
        to = here.off("y", n + 1)
        local = rows_of((to + 2 * core) % 4 * STEP + core * 128, 128)
        band = rows_of(to * STEP + core * 128, 128)
        ah[band, :] = product(local, bh, bl).astype(BF16)
        turned[n] = [here.send(ah.at[band], ah.at[band], c=1 - core)]

    def tally(n):
        to = here.off("y", n + 1)
        arrive(turned[n])
        band = rows_of(to * STEP, STEP)
        rot = dot(x[...], ah[band, :], NT).astype(BF16)
        rot_ref[:, band] = rot
        for p in range(2):
            m = (to * 2 + p) * 8
            res = dot(hot[pl.ds(m, 8)].reshape(8 * CODES, rows), rot[:, p * LANES : (p + 1) * LANES])
            sums = res[:CODES]
            for mm in range(1, 8):
                sums = jnp.where(lane // SUBDIM == mm, res[mm * CODES : (mm + 1) * CODES], sums)
            slab[n, p] = sums
        swap[n] = [here.send(slab.at[n, 1 - core], pair.at[n], c=1 - core)]

    def spray(n):
        to = here.off("y", n + 1)
        arrive(swap[n])
        pair[n] += slab[n, core]
        for k in range(16):
            i, j = here.off("z", k // 4), here.off("x", k % 4)
            block = rows_of((i * 4 + j) * 16, 16)
            if n == 3 and k == 0:
                sums_in[n * 16 + k] = pair[n, block]
            else:
                landed.append(here.send(pair.at[n, block], sums_in.at[n * 16 + k], z=i, x=j, y=to))

    swap, landed = {}, []
    turn(0)
    turn(1)
    tally(0)
    turn(2)
    tally(1)
    spray(0)
    turn(3)
    tally(2)
    spray(1)
    tally(3)
    spray(2)
    spray(3)
    sums = jnp.zeros((16, LANES), F32)
    arrive(landed)
    for n in range(64):
        sums = sums + sums_in[n]
    mean_ref[...] = (sums / count).T
    here.drain()


def per_device(residuals, codes, codebook):
    rows = residuals.shape[0]
    anywhere = pl.BlockSpec(memory_space=pl.ANY)
    vmem = pltpu.VMEM
    matrix = [vmem((D, D), BF16)]
    rotated, mean = pl.pallas_call(
        kernel,
        out_shape=(
            jax.ShapeDtypeStruct((rows, D), BF16),
            jax.ShapeDtypeStruct((LANES, 16), F32),
        ),
        in_specs=[anywhere] * 3,
        out_specs=[pl.BlockSpec(memory_space=pltpu.VMEM)] * 2,
        scratch_shapes=[
            vmem((SUBS, rows), jnp.int32),
            vmem((SUBS, SUBDIM, CODES), BF16),
            vmem((rows, D), BF16),
            vmem((SUBS, CODES, rows), BF16),
            vmem((D, rows), BF16),
            vmem((D, D), F32),
            vmem((D, D), F32),
            vmem((512, D), F32),
            vmem((3, 128, D), F32),
            vmem((15, 8, D), F32),
        ]
        + matrix * 8
        + [
            vmem((4, 2, CODES, LANES), F32),
            vmem((4, CODES, LANES), F32),
            vmem((64, 16, LANES), F32),
            vmem((3, CODES, LANES), F32),
            vmem((4, 64, LANES), F32),
            vmem((4, 16, LANES), F32),
            vmem((3, 16, LANES), F32),
            pltpu.SemaphoreType.DMA((3,)),
            pltpu.SemaphoreType.DMA((400,)),
            pltpu.SemaphoreType.DMA((400,)),
        ],
        compiler_params=pltpu.CompilerParams(
            collective_id=0, has_side_effects=True, vmem_limit_bytes=58 * 2**20
        ),
    )(codes.T, codebook, residuals)
    return rotated, mean.reshape(8, SUBDIM, 16)


def solution(mesh):
    return jax.shard_map(
        per_device,
        mesh=mesh,
        in_specs=(P(("rows", "sub"), None), P(("rows", "sub"), None), P()),
        out_specs=(P(("rows", "sub"), None), P("sub", None, "rows")),
        check_vma=False,
    )
```

```python
import jax
import jax.numpy as jnp
from jax import lax
from jax.experimental import pallas as pl
from jax.experimental.pallas import tpu as pltpu
from jax.sharding import PartitionSpec as P

D = 1024
SUBS = 64
CODES = 256
SUBDIM = 16
LANES = 128
A, B, C = 3.4445, -4.775, 2.0315
MESH = pl.DeviceIdType.MESH
F32 = jnp.float32
BF16 = jnp.bfloat16
NN = (((1,), (0,)), ((), ()))
NT = (((1,), (1,)), ((), ()))
STEP = 256
BANDS = D // STEP
CHUNKS = (
    (0, 128, "z", "xy"),
    (128, 128, "x", "yz"),
    (256, 128, "y", "zx"),
    (384, 128, "z", "xy"),
    (512, 128, "x", "yz"),
    (640, 128, "y", "zx"),
    (768, 128, "z", "xy"),
    (896, 128, "x", "yz"),
)
GROUPS = ((0, 1, 2), (3, 4, 5), (6, 7))
SPLIT = 768


class Here:
    def __init__(self, ssem, rsem):
        rows, sub = lax.axis_index("rows"), lax.axis_index("sub")
        self.at = {"z": rows // 4, "x": rows % 4, "y": sub // 2, "c": sub % 2}
        self.ssem, self.rsem, self.used = ssem, rsem, 0
        self.pending = []

    def device(self, **where):
        at = {**self.at, **where}
        return (at["z"] * 4 + at["x"], at["y"] * 2 + at["c"])

    def off(self, axis, by):
        return (self.at[axis] + by) % 4

    def send(self, src, dst, **where):
        copy = pltpu.make_async_remote_copy(
            src_ref=src,
            dst_ref=dst,
            send_sem=self.ssem.at[self.used],
            recv_sem=self.rsem.at[self.used],
            device_id=self.device(**where),
            device_id_type=MESH,
        )
        self.used += 1
        copy.start()
        self.pending.append(copy)
        return copy

    def greet(self):
        barrier = pltpu.get_barrier_semaphore()

        def signal(**where):
            pl.semaphore_signal(
                barrier, inc=1, device_id=self.device(**where), device_id_type=MESH
            )

        signal(c=1 - self.at["c"])
        for axis in "zxy":
            for j in range(1, 4):
                signal(**{axis: self.off(axis, j)})

    def meet(self):
        pl.semaphore_wait(pltpu.get_barrier_semaphore(), 10)

    def drain(self, some=None):
        done = list(self.pending) if some is None else some
        for copy in done:
            copy.wait_send()
        self.pending = [copy for copy in self.pending if all(copy is not other for other in done)]


def arrive(copies):
    for copy in copies:
        copy.wait_recv()


def rows_of(start, size):
    return pl.ds(pl.multiple_of(start, size), size)


def dot(a, b, dims=NN):
    return lax.dot_general(a, b, dims, preferred_element_type=F32)


def split(value):
    high = value.astype(BF16)
    return high, (value - high.astype(F32)).astype(BF16)


def total_of(value):
    return jnp.sum(jnp.sum(value, axis=0, keepdims=True), axis=1, keepdims=True)


def diagonal():
    row = lax.broadcasted_iota(jnp.int32, (STEP, STEP), 0)
    return row == lax.broadcasted_iota(jnp.int32, (STEP, STEP), 1)


def corner(i, h, l, depth=slice(0, D)):
    band = slice(i * STEP, (i + 1) * STEP)
    mixed = dot(l[band, depth], h[band, depth], NT)
    return dot(h[band, depth], h[band, depth], NT) + (mixed + mixed.T)


def beside(i, rest, h, l, depth=slice(0, D)):
    band = slice(i * STEP, (i + 1) * STEP)
    side = dot(h[band, depth], h[rest, depth], NT)
    return side + (dot(h[band, depth], l[rest, depth], NT) + dot(l[band, depth], h[rest, depth], NT))


def tiles(*bands):
    for i in bands:
        band, rest = slice(i * STEP, (i + 1) * STEP), slice((i + 1) * STEP, D)
        yield i, band, band
        if i < BANDS - 1:
            yield i, band, rest


def tile(i, band, cols, h, l, depth=slice(0, D)):
    return corner(i, h, l, depth) if band == cols else beside(i, cols, h, l, depth)


def store_split(h, l, band, cols, value):
    h[band, cols], l[band, cols] = split(value)
    if band != cols:
        h[cols, band], l[cols, band] = split(value.T)


def kernel(labels_hbm, book_hbm, x_hbm, rot_ref, mean_ref, *scratch):
    (labels, book, x, hot, recon, part, full, got0, got1, got2, ah, al, gh, gl, qh, ql, bh, bl) = scratch[:18]
    (slab, pair, sums_in, counts, countz, countx, county, local, ssem, rsem) = scratch[18:]
    here = Here(ssem, rsem)
    copies = [
        pltpu.make_async_copy(src, dst, local.at[n])
        for n, (src, dst) in enumerate(((labels_hbm, labels), (book_hbm, book), (x_hbm, x)))
    ]
    for copy in copies:
        copy.start()
    here.greet()
    z, xx, y, core = (here.at[a] for a in "zxyc")
    rows = x.shape[0]
    copies[0].wait()
    copies[1].wait()
    levels = lax.broadcasted_iota(jnp.int32, (CODES, rows), 0)

    def rebuild(m, carry):
        one = jnp.where(levels == labels[pl.ds(m, 1), :], 1.0, 0.0).astype(BF16)
        hot[m] = one
        recon[rows_of(m * SUBDIM, SUBDIM), :] = dot(book[m], one).astype(BF16)
        return carry

    lax.fori_loop(0, SUBS, rebuild, 0, unroll=8)
    copies[2].wait()
    here.meet()

    mine, theirs = rows_of(core * 512, 512), rows_of((1 - core) * 512, 512)
    flight, base = {}, {}

    def cols_of(t):
        return pl.ds(CHUNKS[t][0], CHUNKS[t][1])

    def stage_core(t):
        cols = cols_of(t)
        flight[t] = [here.send(part.at[theirs, cols], got0.at[:, cols], c=1 - core)]

    def stage_first(t):
        cols, axis = cols_of(t), CHUNKS[t][2]
        arrive(flight[t])
        part[mine, cols] += got0[:, cols]
        flight[t] = []
        for j in range(1, 4):
            other = here.off(axis, j)
            src = part.at[rows_of(core * 512 + other * 128, 128), cols]
            flight[t].append(here.send(src, got1.at[j - 1, :, cols], **{axis: other}))
        base[t] = core * 512 + here.at[axis] * 128

    def stage_second(t):
        cols, (p, q) = cols_of(t), CHUNKS[t][3]
        arrive(flight[t])
        block = rows_of(base[t], 128)
        part[block, cols] = (part[block, cols] + got1[0, :, cols]) + (got1[1, :, cols] + got1[2, :, cols])
        flight[t] = []
        for n in range(1, 16):
            i, j = here.off(p, n // 4), here.off(q, n % 4)
            src = part.at[rows_of(base[t] + (i * 4 + j) * 8, 8), cols]
            flight[t].append(here.send(src, got2.at[n - 1, :, cols], **{p: i, q: j}))

    def stage_back(t):
        cols, (p, q) = cols_of(t), CHUNKS[t][3]
        arrive(flight[t])
        own = rows_of(base[t] + (here.at[p] * 4 + here.at[q]) * 8, 8)
        total = part[own, cols]
        for n in range(15):
            total = total + got2[n, :, cols]
        full[own, cols] = total
        flight[t] = []
        for n in range(1, 16):
            i, j = here.off(p, n // 4), here.off(q, n % 4)
            flight[t].append(here.send(full.at[own, cols], full.at[own, cols], **{p: i, q: j}))

    def stage_wide(t):
        cols, axis = cols_of(t), CHUNKS[t][2]
        arrive(flight[t])
        block = rows_of(base[t], 128)
        flight[t] = []
        for j in range(1, 4):
            other = here.off(axis, j)
            flight[t].append(here.send(full.at[block, cols], full.at[block, cols], **{axis: other}))

    def stage_last(t):
        cols = cols_of(t)
        arrive(flight[t])
        flight[t] = [here.send(full.at[mine, cols], full.at[mine, cols], c=1 - core)]

    for first in range(0, D, STEP):
        cols = pl.ds(first, STEP)
        part[:, cols] = dot(recon[...], x[:, cols])
        for t in range(len(CHUNKS)):
            if first <= CHUNKS[t][0] < first + STEP:
                stage_core(t)
    for t in range(len(CHUNKS)):
        stage_first(t)

    lane = lax.broadcasted_iota(jnp.int32, (CODES, LANES), 1)
    ones = jnp.ones((rows, LANES), BF16)
    counts[0] = jnp.zeros((CODES, LANES), F32)

    def count(g, carry):
        value = counts[0]
        for mm in range(8):
            m = g * 8 + mm
            value = jnp.where(lane == m, dot(hot[m], ones), value)
        counts[0] = value
        return carry

    lax.fori_loop(0, 3, count, 0)
    def go(stage, g):
        for t in GROUPS[g]:
            stage(t)

    for t in GROUPS[0]:
        arrive(flight[t])
        flight[t] = []
    go(stage_second, 0)
    lax.fori_loop(3, 7, count, 0)
    go(stage_second, 1)
    lax.fori_loop(7, 8, count, 0)
    count_flight = [here.send(counts.at[0], counts.at[1], c=1 - core)]
    go(stage_back, 0)
    go(stage_second, 2)
    reads_part = list(here.pending)
    arrive(count_flight)
    counts[2] = counts[0] + counts[1]
    count_flight = []
    for j in range(1, 4):
        other = here.off("z", j)
        src = counts.at[2, rows_of(other * 64, 64)]
        count_flight.append(here.send(src, countz.at[j - 1], z=other))
    go(stage_back, 1)
    go(stage_wide, 0)
    go(stage_back, 2)
    arrive(count_flight)
    countz[3] = (counts[2, rows_of(z * 64, 64)] + countz[0]) + (countz[1] + countz[2])
    count_flight = []
    for j in range(1, 4):
        other = here.off("x", j)
        count_flight.append(here.send(countz.at[3, rows_of(other * 16, 16)], countx.at[j - 1], x=other))
    go(stage_wide, 1)
    go(stage_wide, 2)
    go(stage_last, 0)
    go(stage_last, 1)
    arrive(count_flight)
    countx[3] = (countz[3, rows_of(xx * 16, 16)] + countx[0]) + (countx[1] + countx[2])
    count_flight = []
    for j in range(1, 4):
        count_flight.append(here.send(countx.at[3], county.at[j - 1], y=here.off("y", j)))
    for t in GROUPS[0] + GROUPS[1]:
        arrive(flight[t])

    def load(cols):
        def one(i, carry):
            band = rows_of(i * 64, 64)
            ah[band, cols], al[band, cols] = split(full[rows_of((i * 64 + core * 512) % D, 64), cols])
            return carry

        lax.fori_loop(0, D // 64, one, 0)

    load(slice(0, SPLIT))
    here.drain(reads_part)
    go(stage_last, 2)
    for i, band, cols in tiles(0, 1, 2, 3):
        part[band, cols] = tile(i, band, cols, ah, al, slice(0, SPLIT))
    for t in GROUPS[2]:
        arrive(flight[t])
    load(slice(SPLIT, D))
    trace, square = jnp.zeros((1, 1), F32), jnp.zeros((1, 1), F32)
    for i, band, cols in tiles(0, 1, 2, 3):
        value = tile(i, band, cols, ah, al, slice(SPLIT, D)) + part[band, cols]
        if band == cols:
            trace += total_of(jnp.where(diagonal(), value, 0.0))
            square += total_of(value * value)
        else:
            square += 2.0 * total_of(value * value)
        part[band, cols] = value
        store_split(gh, gl, band, cols, value)

    norm = 1.0 / (trace + 1e-06)
    scale = jnp.sqrt(jnp.sqrt(square * norm * norm + 1e-06))
    unit = norm / (scale * scale)
    front = jnp.sqrt(norm) / scale

    def polynomial(front, unit):
        cb, cc = B * front * unit, C * front * unit
        for i, band, cols in tiles(0, 1, 2, 3):
            value = cb * part[band, cols] + cc * (unit * tile(i, band, cols, gh, gl))
            if band == cols:
                value = value + jnp.where(diagonal(), A * front, 0.0)
            store_split(qh, ql, band, cols, value)

    def product(band, h, l):
        return dot(qh[band, :], h[...]) + (dot(qh[band, :], l[...]) + dot(ql[band, :], h[...]))

    polynomial(front, unit)

    halves = []
    for i in range(2):
        band, there = slice(i * STEP, (i + 1) * STEP), slice(512 + i * STEP, 512 + (i + 1) * STEP)
        bh[band, :], bl[band, :] = split(product(band, ah, al))
        halves.append(here.send(bh.at[band], bh.at[there], c=1 - core))
        halves.append(here.send(bl.at[band], bl.at[there], c=1 - core))

    def gram(i, band, cols):
        value = tile(i, band, cols, bh, bl)
        part[band, cols] = value
        store_split(gh, gl, band, cols, value)

    low, high, right = slice(0, STEP), slice(STEP, 512), slice(512, D)
    gram(0, low, low)
    gram(0, low, high)
    gram(1, high, high)
    arrive(halves)
    gram(0, low, right)
    gram(1, high, right)
    for i, band, cols in tiles(2, 3):
        gram(i, band, cols)
    one = jnp.ones((1, 1), F32)
    polynomial(one, one)

    arrive(count_flight)
    count = (countx[3] + county[0]) + (county[1] + county[2])
    row = lax.broadcasted_iota(jnp.int32, (LANES, LANES), 0)
    col = lax.broadcasted_iota(jnp.int32, (LANES, LANES), 1)
    spread = jnp.where(row == (y * 2 + core) * 8 + col // SUBDIM, 1.0, 0.0)
    count = jnp.dot(count, spread, precision=lax.Precision.HIGHEST, preferred_element_type=F32)

    turned = {}

    def turn(pair_of_bands):
        to = here.off("y", 2 * pair_of_bands + core + 1)
        local = rows_of((to + 2 * core) % 4 * STEP, STEP)
        band = rows_of(to * STEP, STEP)
        ah[band, :] = product(local, bh, bl).astype(BF16)
        turned[pair_of_bands] = [here.send(ah.at[band], ah.at[band], c=1 - core)]

    def tally(n):
        to = here.off("y", n + 1)
        if n % 2 == 0:
            arrive(turned[n // 2])
        band = rows_of(to * STEP, STEP)
        rot = dot(x[...], ah[band, :], NT).astype(BF16)
        rot_ref[:, band] = rot
        for p in range(2):
            m = (to * 2 + p) * 8
            res = dot(hot[pl.ds(m, 8)].reshape(8 * CODES, rows), rot[:, p * LANES : (p + 1) * LANES])
            sums = res[:CODES]
            for mm in range(1, 8):
                sums = jnp.where(lane // SUBDIM == mm, res[mm * CODES : (mm + 1) * CODES], sums)
            slab[n, p] = sums
        swap[n] = [here.send(slab.at[n, 1 - core], pair.at[n], c=1 - core)]

    def spray(n):
        to = here.off("y", n + 1)
        arrive(swap[n])
        pair[n] += slab[n, core]
        for k in range(16):
            i, j = here.off("z", k // 4), here.off("x", k % 4)
            block = rows_of((i * 4 + j) * 16, 16)
            if n == 3 and k == 0:
                sums_in[n * 16 + k] = pair[n, block]
            else:
                landed.append(here.send(pair.at[n, block], sums_in.at[n * 16 + k], z=i, x=j, y=to))

    swap, landed = {}, []
    turn(0)
    turn(1)
    tally(0)
    tally(1)
    spray(0)
    tally(2)
    spray(1)
    tally(3)
    spray(2)
    spray(3)
    sums = jnp.zeros((16, LANES), F32)
    arrive(landed)
    for n in range(64):
        sums = sums + sums_in[n]
    mean_ref[...] = (sums / count).T
    here.drain()


def per_device(residuals, codes, codebook):
    rows = residuals.shape[0]
    anywhere = pl.BlockSpec(memory_space=pltpu.HBM)
    vmem = pltpu.VMEM
    matrix = [vmem((D, D), BF16)]
    rotated, mean = pl.pallas_call(
        kernel,
        out_shape=(
            jax.ShapeDtypeStruct((rows, D), BF16),
            jax.ShapeDtypeStruct((LANES, 16), F32),
        ),
        in_specs=[anywhere] * 3,
        out_specs=[pl.BlockSpec(memory_space=pltpu.VMEM)] * 2,
        scratch_shapes=[
            vmem((SUBS, rows), jnp.int32),
            vmem((SUBS, SUBDIM, CODES), BF16),
            vmem((rows, D), BF16),
            vmem((SUBS, CODES, rows), BF16),
            vmem((D, rows), BF16),
            vmem((D, D), F32),
            vmem((D, D), F32),
            vmem((512, D), F32),
            vmem((3, 128, D), F32),
            vmem((15, 8, D), F32),
        ]
        + matrix * 8
        + [
            vmem((4, 2, CODES, LANES), F32),
            vmem((4, CODES, LANES), F32),
            vmem((64, 16, LANES), F32),
            vmem((3, CODES, LANES), F32),
            vmem((4, 64, LANES), F32),
            vmem((4, 16, LANES), F32),
            vmem((3, 16, LANES), F32),
            pltpu.SemaphoreType.DMA((3,)),
            pltpu.SemaphoreType.DMA((400,)),
            pltpu.SemaphoreType.DMA((400,)),
        ],
        compiler_params=pltpu.CompilerParams(
            collective_id=0, has_side_effects=True, vmem_limit_bytes=52 * 2**20
        ),
    )(codes.T, codebook, residuals)
    return rotated, mean.reshape(8, SUBDIM, 16)


def solution(mesh):
    return jax.shard_map(
        per_device,
        mesh=mesh,
        in_specs=(P(("rows", "sub"), None), P(("rows", "sub"), None), P()),
        out_specs=(P(("rows", "sub"), None), P("sub", None, "rows")),
        check_vma=False,
    )
```

```python
import jax
import jax.numpy as jnp
from jax import lax
from jax.experimental import pallas as pl
from jax.experimental.pallas import tpu as pltpu
from jax.sharding import PartitionSpec as P

D = 1024
SUBS = 64
CODES = 256
SUBDIM = 16
LANES = 128
A, B, C = 3.4445, -4.775, 2.0315
MESH = pl.DeviceIdType.MESH
F32 = jnp.float32
BF16 = jnp.bfloat16
NN = (((1,), (0,)), ((), ()))
NT = (((1,), (1,)), ((), ()))
STEP = 256
BANDS = D // STEP
CHUNKS = (
    (0, 128, "z", "xy"),
    (128, 128, "x", "yz"),
    (256, 128, "y", "zx"),
    (384, 128, "z", "xy"),
    (512, 128, "x", "yz"),
    (640, 128, "y", "zx"),
    (768, 128, "z", "xy"),
    (896, 128, "x", "yz"),
)
GROUPS = ((0, 1, 2), (3, 4, 5), (6, 7))
SPLIT = 768


class Here:
    def __init__(self, ssem, rsem):
        rows, sub = lax.axis_index("rows"), lax.axis_index("sub")
        self.at = {"z": rows // 4, "x": rows % 4, "y": sub // 2, "c": sub % 2}
        self.ssem, self.rsem, self.used = ssem, rsem, 0
        self.pending = []

    def device(self, **where):
        at = {**self.at, **where}
        return (at["z"] * 4 + at["x"], at["y"] * 2 + at["c"])

    def off(self, axis, by):
        return (self.at[axis] + by) % 4

    def send(self, src, dst, **where):
        copy = pltpu.make_async_remote_copy(
            src_ref=src,
            dst_ref=dst,
            send_sem=self.ssem.at[self.used],
            recv_sem=self.rsem.at[self.used],
            device_id=self.device(**where),
            device_id_type=MESH,
        )
        self.used += 1
        copy.start()
        self.pending.append(copy)
        return copy

    def greet(self):
        barrier = pltpu.get_barrier_semaphore()

        def signal(**where):
            pl.semaphore_signal(
                barrier, inc=1, device_id=self.device(**where), device_id_type=MESH
            )

        signal(c=1 - self.at["c"])
        for axis in "zxy":
            for j in range(1, 4):
                signal(**{axis: self.off(axis, j)})

    def meet(self):
        pl.semaphore_wait(pltpu.get_barrier_semaphore(), 10)

    def drain(self, some=None):
        done = list(self.pending) if some is None else some
        for copy in done:
            copy.wait_send()
        self.pending = [copy for copy in self.pending if all(copy is not other for other in done)]


def arrive(copies):
    for copy in copies:
        copy.wait_recv()


def rows_of(start, size):
    return pl.ds(pl.multiple_of(start, size), size)


def dot(a, b, dims=NN):
    return lax.dot_general(a, b, dims, preferred_element_type=F32)


def split(value):
    high = value.astype(BF16)
    return high, (value - high.astype(F32)).astype(BF16)


def total_of(value):
    return jnp.sum(jnp.sum(value, axis=0, keepdims=True), axis=1, keepdims=True)


def diagonal():
    row = lax.broadcasted_iota(jnp.int32, (STEP, STEP), 0)
    return row == lax.broadcasted_iota(jnp.int32, (STEP, STEP), 1)


def corner(i, h, l, depth=slice(0, D)):
    band = slice(i * STEP, (i + 1) * STEP)
    mixed = dot(l[band, depth], h[band, depth], NT)
    return dot(h[band, depth], h[band, depth], NT) + (mixed + mixed.T)


def beside(i, rest, h, l, depth=slice(0, D)):
    band = slice(i * STEP, (i + 1) * STEP)
    side = dot(h[band, depth], h[rest, depth], NT)
    return side + (dot(h[band, depth], l[rest, depth], NT) + dot(l[band, depth], h[rest, depth], NT))


def tiles(*bands):
    for i in bands:
        band, rest = slice(i * STEP, (i + 1) * STEP), slice((i + 1) * STEP, D)
        yield i, band, band
        if i < BANDS - 1:
            yield i, band, rest


def tile(i, band, cols, h, l, depth=slice(0, D)):
    return corner(i, h, l, depth) if band == cols else beside(i, cols, h, l, depth)


def store_split(h, l, band, cols, value):
    h[band, cols], l[band, cols] = split(value)
    if band != cols:
        h[cols, band], l[cols, band] = split(value.T)


def kernel(labels_hbm, book_hbm, x_hbm, rot_ref, mean_ref, *scratch):
    (labels, book, x, hot, recon, part, full, got0, got1, got2, ah, al, gh, gl, qh, ql, bh, bl) = scratch[:18]
    (slab, pair, sums_in, counts, countz, countx, county, local, ssem, rsem) = scratch[18:]
    here = Here(ssem, rsem)
    copies = [
        pltpu.make_async_copy(src, dst, local.at[n])
        for n, (src, dst) in enumerate(((labels_hbm, labels), (book_hbm, book), (x_hbm, x)))
    ]
    for copy in copies:
        copy.start()
    here.greet()
    z, xx, y, core = (here.at[a] for a in "zxyc")
    rows = x.shape[0]
    copies[0].wait()
    copies[1].wait()
    levels = lax.broadcasted_iota(jnp.int32, (CODES, rows), 0)

    def rebuild(m, carry):
        one = jnp.where(levels == labels[pl.ds(m, 1), :], 1.0, 0.0).astype(BF16)
        hot[m] = one
        recon[rows_of(m * SUBDIM, SUBDIM), :] = dot(book[m], one).astype(BF16)
        return carry

    lax.fori_loop(0, SUBS, rebuild, 0, unroll=8)
    copies[2].wait()
    here.meet()

    mine, theirs = rows_of(core * 512, 512), rows_of((1 - core) * 512, 512)
    flight, base = {}, {}

    def cols_of(t):
        return pl.ds(CHUNKS[t][0], CHUNKS[t][1])

    def stage_core(t):
        cols = cols_of(t)
        flight[t] = [here.send(part.at[theirs, cols], got0.at[:, cols], c=1 - core)]

    def stage_first(t):
        cols, axis = cols_of(t), CHUNKS[t][2]
        arrive(flight[t])
        part[mine, cols] += got0[:, cols]
        flight[t] = []
        for j in range(1, 4):
            other = here.off(axis, j)
            src = part.at[rows_of(core * 512 + other * 128, 128), cols]
            flight[t].append(here.send(src, got1.at[j - 1, :, cols], **{axis: other}))
        base[t] = core * 512 + here.at[axis] * 128

    def stage_second(t):
        cols, (p, q) = cols_of(t), CHUNKS[t][3]
        arrive(flight[t])
        block = rows_of(base[t], 128)
        part[block, cols] = (part[block, cols] + got1[0, :, cols]) + (got1[1, :, cols] + got1[2, :, cols])
        flight[t] = []
        for n in range(1, 16):
            i, j = here.off(p, n // 4), here.off(q, n % 4)
            src = part.at[rows_of(base[t] + (i * 4 + j) * 8, 8), cols]
            flight[t].append(here.send(src, got2.at[n - 1, :, cols], **{p: i, q: j}))

    def stage_back(t):
        cols, (p, q) = cols_of(t), CHUNKS[t][3]
        arrive(flight[t])
        own = rows_of(base[t] + (here.at[p] * 4 + here.at[q]) * 8, 8)
        total = part[own, cols]
        for n in range(15):
            total = total + got2[n, :, cols]
        full[own, cols] = total
        flight[t] = []
        for n in range(1, 16):
            i, j = here.off(p, n // 4), here.off(q, n % 4)
            flight[t].append(here.send(full.at[own, cols], full.at[own, cols], **{p: i, q: j}))

    def stage_wide(t):
        cols, axis = cols_of(t), CHUNKS[t][2]
        arrive(flight[t])
        block = rows_of(base[t], 128)
        flight[t] = []
        for j in range(1, 4):
            other = here.off(axis, j)
            flight[t].append(here.send(full.at[block, cols], full.at[block, cols], **{axis: other}))

    def stage_last(t):
        cols = cols_of(t)
        arrive(flight[t])
        flight[t] = [here.send(full.at[mine, cols], full.at[mine, cols], c=1 - core)]

    for first in range(0, D, STEP):
        cols = pl.ds(first, STEP)
        part[:, cols] = dot(recon[...], x[:, cols])
        for t in range(len(CHUNKS)):
            if first <= CHUNKS[t][0] < first + STEP:
                stage_core(t)
    for t in range(len(CHUNKS)):
        stage_first(t)

    lane = lax.broadcasted_iota(jnp.int32, (CODES, LANES), 1)
    ones = jnp.ones((rows, LANES), BF16)
    counts[0] = jnp.zeros((CODES, LANES), F32)

    def count(g, carry):
        value = counts[0]
        for mm in range(8):
            m = g * 8 + mm
            value = jnp.where(lane == m, dot(hot[m], ones), value)
        counts[0] = value
        return carry

    lax.fori_loop(0, 3, count, 0)
    def go(stage, g):
        for t in GROUPS[g]:
            stage(t)

    for t in GROUPS[0]:
        arrive(flight[t])
        flight[t] = []
    go(stage_second, 0)
    lax.fori_loop(3, 7, count, 0)
    go(stage_second, 1)
    lax.fori_loop(7, 8, count, 0)
    count_flight = [here.send(counts.at[0], counts.at[1], c=1 - core)]
    go(stage_back, 0)
    go(stage_second, 2)
    reads_part = list(here.pending)
    arrive(count_flight)
    counts[2] = counts[0] + counts[1]
    count_flight = []
    for j in range(1, 4):
        other = here.off("z", j)
        src = counts.at[2, rows_of(other * 64, 64)]
        count_flight.append(here.send(src, countz.at[j - 1], z=other))
    go(stage_back, 1)
    go(stage_wide, 0)
    go(stage_back, 2)
    arrive(count_flight)
    countz[3] = (counts[2, rows_of(z * 64, 64)] + countz[0]) + (countz[1] + countz[2])
    count_flight = []
    for j in range(1, 4):
        other = here.off("x", j)
        count_flight.append(here.send(countz.at[3, rows_of(other * 16, 16)], countx.at[j - 1], x=other))
    go(stage_wide, 1)
    go(stage_wide, 2)
    go(stage_last, 0)
    go(stage_last, 1)
    arrive(count_flight)
    countx[3] = (countz[3, rows_of(xx * 16, 16)] + countx[0]) + (countx[1] + countx[2])
    count_flight = []
    for j in range(1, 4):
        count_flight.append(here.send(countx.at[3], county.at[j - 1], y=here.off("y", j)))
    for t in GROUPS[0] + GROUPS[1]:
        arrive(flight[t])

    def load(cols):
        def one(i, carry):
            band = rows_of(i * 64, 64)
            ah[band, cols], al[band, cols] = split(full[rows_of((i * 64 + core * 512) % D, 64), cols])
            return carry

        lax.fori_loop(0, D // 64, one, 0)

    load(slice(0, SPLIT))
    here.drain(reads_part)
    go(stage_last, 2)
    for i, band, cols in tiles(0, 1, 2, 3):
        part[band, cols] = tile(i, band, cols, ah, al, slice(0, SPLIT))
    for t in GROUPS[2]:
        arrive(flight[t])
    load(slice(SPLIT, D))
    trace, square = jnp.zeros((1, 1), F32), jnp.zeros((1, 1), F32)
    for i, band, cols in tiles(0, 1, 2, 3):
        value = tile(i, band, cols, ah, al, slice(SPLIT, D)) + part[band, cols]
        if band == cols:
            trace += total_of(jnp.where(diagonal(), value, 0.0))
            square += total_of(value * value)
        else:
            square += 2.0 * total_of(value * value)
        part[band, cols] = value
        store_split(gh, gl, band, cols, value)

    norm = 1.0 / (trace + 1e-06)
    scale = jnp.sqrt(jnp.sqrt(square * norm * norm + 1e-06))
    unit = norm / (scale * scale)
    front = jnp.sqrt(norm) / scale

    def polynomial(front, unit):
        cb, cc = B * front * unit, C * front * unit
        for i, band, cols in tiles(0, 1, 2, 3):
            value = cb * part[band, cols] + cc * (unit * tile(i, band, cols, gh, gl))
            if band == cols:
                value = value + jnp.where(diagonal(), A * front, 0.0)
            store_split(qh, ql, band, cols, value)

    def product(band, h, l):
        return dot(qh[band, :], h[...]) + (dot(qh[band, :], l[...]) + dot(ql[band, :], h[...]))

    polynomial(front, unit)

    halves = []
    for i in range(2):
        band, there = slice(i * STEP, (i + 1) * STEP), slice(512 + i * STEP, 512 + (i + 1) * STEP)
        bh[band, :], bl[band, :] = split(product(band, ah, al))
        halves.append(here.send(bh.at[band], bh.at[there], c=1 - core))
        halves.append(here.send(bl.at[band], bl.at[there], c=1 - core))

    def gram(i, band, cols):
        value = tile(i, band, cols, bh, bl)
        part[band, cols] = value
        store_split(gh, gl, band, cols, value)

    low, high, right = slice(0, STEP), slice(STEP, 512), slice(512, D)
    gram(0, low, low)
    gram(0, low, high)
    gram(1, high, high)
    arrive(halves)
    gram(0, low, right)
    gram(1, high, right)
    for i, band, cols in tiles(2, 3):
        gram(i, band, cols)
    one = jnp.ones((1, 1), F32)
    polynomial(one, one)

    arrive(count_flight)
    count = (countx[3] + county[0]) + (county[1] + county[2])
    row = lax.broadcasted_iota(jnp.int32, (LANES, LANES), 0)
    col = lax.broadcasted_iota(jnp.int32, (LANES, LANES), 1)
    spread = jnp.where(row == (y * 2 + core) * 8 + col // SUBDIM, 1.0, 0.0)
    count = jnp.dot(count, spread, precision=lax.Precision.HIGHEST, preferred_element_type=F32)

    turned = {}

    def turn(pair_of_bands):
        to = here.off("y", 2 * pair_of_bands + core + 1)
        local = rows_of((to + 2 * core) % 4 * STEP, STEP)
        band = rows_of(to * STEP, STEP)
        ah[band, :] = product(local, bh, bl).astype(BF16)
        turned[pair_of_bands] = [here.send(ah.at[band], ah.at[band], c=1 - core)]

    def tally(n):
        to = here.off("y", n + 1)
        if n % 2 == 0:
            arrive(turned[n // 2])
        band = rows_of(to * STEP, STEP)
        rot = dot(x[...], ah[band, :], NT).astype(BF16)
        rot_ref[:, band] = rot
        for p in range(2):
            m = (to * 2 + p) * 8
            res = dot(hot[pl.ds(m, 8)].reshape(8 * CODES, rows), rot[:, p * LANES : (p + 1) * LANES])
            sums = res[:CODES]
            for mm in range(1, 8):
                sums = jnp.where(lane // SUBDIM == mm, res[mm * CODES : (mm + 1) * CODES], sums)
            slab[n, p] = sums
        swap[n] = [here.send(slab.at[n, 1 - core], pair.at[n], c=1 - core)]

    def spray(n):
        to = here.off("y", n + 1)
        arrive(swap[n])
        pair[n] += slab[n, core]
        for k in range(16):
            i, j = here.off("z", k // 4), here.off("x", k % 4)
            block = rows_of((i * 4 + j) * 16, 16)
            if n == 3 and k == 0:
                sums_in[n * 16 + k] = pair[n, block]
            else:
                landed.append(here.send(pair.at[n, block], sums_in.at[n * 16 + k], z=i, x=j, y=to))

    swap, landed = {}, []
    turn(0)
    turn(1)
    tally(0)
    tally(1)
    spray(0)
    tally(2)
    spray(1)
    tally(3)
    spray(2)
    spray(3)
    sums = jnp.zeros((16, LANES), F32)
    arrive(landed)
    for n in range(64):
        sums = sums + sums_in[n]
    mean_ref[...] = (sums / count).T
    here.drain()


def per_device(residuals, codes, codebook):
    rows = residuals.shape[0]
    anywhere = pl.BlockSpec(memory_space=pltpu.HBM)
    vmem = pltpu.VMEM
    matrix = [vmem((D, D), BF16)]
    rotated, mean = pl.pallas_call(
        kernel,
        out_shape=(
            jax.ShapeDtypeStruct((rows, D), BF16),
            jax.ShapeDtypeStruct((LANES, 16), F32),
        ),
        in_specs=[anywhere] * 3,
        out_specs=[pl.BlockSpec(memory_space=pltpu.VMEM)] * 2,
        scratch_shapes=[
            vmem((SUBS, rows), jnp.int32),
            vmem((SUBS, SUBDIM, CODES), BF16),
            vmem((rows, D), BF16),
            vmem((SUBS, CODES, rows), BF16),
            vmem((D, rows), BF16),
            vmem((D, D), F32),
            vmem((D, D), F32),
            vmem((512, D), F32),
            vmem((3, 128, D), F32),
            vmem((15, 8, D), F32),
        ]
        + matrix * 8
        + [
            vmem((4, 2, CODES, LANES), F32),
            vmem((4, CODES, LANES), F32),
            vmem((64, 16, LANES), F32),
            vmem((3, CODES, LANES), F32),
            vmem((4, 64, LANES), F32),
            vmem((4, 16, LANES), F32),
            vmem((3, 16, LANES), F32),
            pltpu.SemaphoreType.DMA((3,)),
            pltpu.SemaphoreType.DMA((400,)),
            pltpu.SemaphoreType.DMA((400,)),
        ],
        compiler_params=pltpu.CompilerParams(
            collective_id=0, has_side_effects=True, vmem_limit_bytes=52 * 2**20
        ),
    )(*(pltpu.with_memory_space_constraint(a, pltpu.HBM) for a in (codes.T, codebook, residuals)))
    return rotated, mean.reshape(8, SUBDIM, 16)


def solution(mesh):
    return jax.shard_map(
        per_device,
        mesh=mesh,
        in_specs=(P(("rows", "sub"), None), P(("rows", "sub"), None), P()),
        out_specs=(P(("rows", "sub"), None), P("sub", None, "rows")),
        check_vma=False,
    )
```

```python
import jax
import jax.numpy as jnp
from jax import lax
from jax.experimental import pallas as pl
from jax.experimental.pallas import tpu as pltpu
from jax.sharding import PartitionSpec as P

D = 1024
SUBS = 64
CODES = 256
SUBDIM = 16
LANES = 128
A, B, C = 3.4445, -4.775, 2.0315
MESH = pl.DeviceIdType.MESH
F32 = jnp.float32
BF16 = jnp.bfloat16
NN = (((1,), (0,)), ((), ()))
NT = (((1,), (1,)), ((), ()))
STEP = 256
BANDS = D // STEP
CHUNKS = (
    (0, 128, "z", "xy"),
    (128, 128, "x", "yz"),
    (256, 128, "y", "zx"),
    (384, 128, "z", "xy"),
    (512, 128, "x", "yz"),
    (640, 128, "y", "zx"),
    (768, 128, "z", "xy"),
    (896, 128, "x", "yz"),
)
GROUPS = ((0, 1, 2), (3, 4, 5), (6, 7))
SPLIT = 768


class Here:
    def __init__(self, ssem, rsem):
        rows, sub = lax.axis_index("rows"), lax.axis_index("sub")
        self.at = {"z": rows // 4, "x": rows % 4, "y": sub // 2, "c": sub % 2}
        self.ssem, self.rsem, self.used = ssem, rsem, 0
        self.pending = []

    def device(self, **where):
        at = {**self.at, **where}
        return (at["z"] * 4 + at["x"], at["y"] * 2 + at["c"])

    def off(self, axis, by):
        return (self.at[axis] + by) % 4

    def send(self, src, dst, **where):
        copy = pltpu.make_async_remote_copy(
            src_ref=src,
            dst_ref=dst,
            send_sem=self.ssem.at[self.used],
            recv_sem=self.rsem.at[self.used],
            device_id=self.device(**where),
            device_id_type=MESH,
        )
        self.used += 1
        copy.start()
        self.pending.append(copy)
        return copy

    def greet(self):
        barrier = pltpu.get_barrier_semaphore()

        def signal(**where):
            pl.semaphore_signal(
                barrier, inc=1, device_id=self.device(**where), device_id_type=MESH
            )

        signal(c=1 - self.at["c"])
        for axis in "zxy":
            for j in range(1, 4):
                signal(**{axis: self.off(axis, j)})

    def meet(self):
        pl.semaphore_wait(pltpu.get_barrier_semaphore(), 10)

    def drain(self, some=None):
        done = list(self.pending) if some is None else some
        for copy in done:
            copy.wait_send()
        self.pending = [copy for copy in self.pending if all(copy is not other for other in done)]


def arrive(copies):
    for copy in copies:
        copy.wait_recv()


def rows_of(start, size):
    return pl.ds(pl.multiple_of(start, size), size)


def dot(a, b, dims=NN):
    return lax.dot_general(a, b, dims, preferred_element_type=F32)


def split(value):
    high = value.astype(BF16)
    return high, (value - high.astype(F32)).astype(BF16)


def total_of(value):
    return jnp.sum(jnp.sum(value, axis=0, keepdims=True), axis=1, keepdims=True)


def diagonal():
    row = lax.broadcasted_iota(jnp.int32, (STEP, STEP), 0)
    return row == lax.broadcasted_iota(jnp.int32, (STEP, STEP), 1)


def corner(i, h, l, depth=slice(0, D)):
    band = slice(i * STEP, (i + 1) * STEP)
    mixed = dot(l[band, depth], h[band, depth], NT)
    return dot(h[band, depth], h[band, depth], NT) + (mixed + mixed.T)


def beside(i, rest, h, l, depth=slice(0, D)):
    band = slice(i * STEP, (i + 1) * STEP)
    side = dot(h[band, depth], h[rest, depth], NT)
    return side + (dot(h[band, depth], l[rest, depth], NT) + dot(l[band, depth], h[rest, depth], NT))


def tiles(*bands):
    for i in bands:
        band, rest = slice(i * STEP, (i + 1) * STEP), slice((i + 1) * STEP, D)
        yield i, band, band
        if i < BANDS - 1:
            yield i, band, rest


def tile(i, band, cols, h, l, depth=slice(0, D)):
    return corner(i, h, l, depth) if band == cols else beside(i, cols, h, l, depth)


def store_split(h, l, band, cols, value):
    h[band, cols], l[band, cols] = split(value)
    if band != cols:
        h[cols, band], l[cols, band] = split(value.T)


def kernel(labels_hbm, book_hbm, x_hbm, rot_ref, mean_ref, *scratch):
    (labels, book, x, hot, recon, part, full, got0, got1, got2, ah, al, gh, gl, qh, ql, bh, bl) = scratch[:18]
    (slab, pair, sums_in, counts, countz, countx, county, local, ssem, rsem) = scratch[18:]
    here = Here(ssem, rsem)
    copies = [
        pltpu.make_async_copy(src, dst, local.at[n])
        for n, (src, dst) in enumerate(((labels_hbm, labels), (book_hbm, book), (x_hbm, x)))
    ]
    for copy in copies:
        copy.start()
    here.greet()
    z, xx, y, core = (here.at[a] for a in "zxyc")
    rows = x.shape[0]
    copies[0].wait()
    copies[1].wait()
    levels = lax.broadcasted_iota(jnp.int32, (CODES, rows), 0)

    def rebuild(m, carry):
        one = jnp.where(levels == labels[pl.ds(m, 1), :], 1.0, 0.0).astype(BF16)
        hot[m] = one
        recon[rows_of(m * SUBDIM, SUBDIM), :] = dot(book[m], one).astype(BF16)
        return carry

    lax.fori_loop(0, SUBS, rebuild, 0, unroll=8)
    copies[2].wait()

    mine, theirs = rows_of(core * 512, 512), rows_of((1 - core) * 512, 512)
    flight, base = {}, {}

    def cols_of(t):
        return pl.ds(CHUNKS[t][0], CHUNKS[t][1])

    def stage_core(t):
        cols = cols_of(t)
        flight[t] = [here.send(part.at[theirs, cols], got0.at[:, cols], c=1 - core)]

    def stage_first(t):
        cols, axis = cols_of(t), CHUNKS[t][2]
        arrive(flight[t])
        part[mine, cols] += got0[:, cols]
        flight[t] = []
        for j in range(1, 4):
            other = here.off(axis, j)
            src = part.at[rows_of(core * 512 + other * 128, 128), cols]
            flight[t].append(here.send(src, got1.at[j - 1, :, cols], **{axis: other}))
        base[t] = core * 512 + here.at[axis] * 128

    def stage_second(t):
        cols, (p, q) = cols_of(t), CHUNKS[t][3]
        arrive(flight[t])
        block = rows_of(base[t], 128)
        part[block, cols] = (part[block, cols] + got1[0, :, cols]) + (got1[1, :, cols] + got1[2, :, cols])
        flight[t] = []
        for n in range(1, 16):
            i, j = here.off(p, n // 4), here.off(q, n % 4)
            src = part.at[rows_of(base[t] + (i * 4 + j) * 8, 8), cols]
            flight[t].append(here.send(src, got2.at[n - 1, :, cols], **{p: i, q: j}))

    def stage_back(t):
        cols, (p, q) = cols_of(t), CHUNKS[t][3]
        arrive(flight[t])
        own = rows_of(base[t] + (here.at[p] * 4 + here.at[q]) * 8, 8)
        total = part[own, cols]
        for n in range(15):
            total = total + got2[n, :, cols]
        full[own, cols] = total
        flight[t] = []
        for n in range(1, 16):
            i, j = here.off(p, n // 4), here.off(q, n % 4)
            flight[t].append(here.send(full.at[own, cols], full.at[own, cols], **{p: i, q: j}))

    def stage_wide(t):
        cols, axis = cols_of(t), CHUNKS[t][2]
        arrive(flight[t])
        block = rows_of(base[t], 128)
        flight[t] = []
        for j in range(1, 4):
            other = here.off(axis, j)
            flight[t].append(here.send(full.at[block, cols], full.at[block, cols], **{axis: other}))

    def stage_last(t):
        cols = cols_of(t)
        arrive(flight[t])
        flight[t] = [here.send(full.at[mine, cols], full.at[mine, cols], c=1 - core)]

    for first in range(0, D, STEP):
        cols = pl.ds(first, STEP)
        part[:, cols] = dot(recon[...], x[:, cols])
        if first == 0:
            here.meet()
        for t in range(len(CHUNKS)):
            if first <= CHUNKS[t][0] < first + STEP:
                stage_core(t)
    for t in range(len(CHUNKS)):
        stage_first(t)

    lane = lax.broadcasted_iota(jnp.int32, (CODES, LANES), 1)
    ones = jnp.ones((rows, LANES), BF16)
    counts[0] = jnp.zeros((CODES, LANES), F32)

    def count(g, carry):
        value = counts[0]
        for mm in range(8):
            m = g * 8 + mm
            value = jnp.where(lane == m, dot(hot[m], ones), value)
        counts[0] = value
        return carry

    lax.fori_loop(0, 3, count, 0)
    def go(stage, g):
        for t in GROUPS[g]:
            stage(t)

    for t in GROUPS[0]:
        arrive(flight[t])
        flight[t] = []
    go(stage_second, 0)
    lax.fori_loop(3, 7, count, 0)
    go(stage_second, 1)
    lax.fori_loop(7, 8, count, 0)
    count_flight = [here.send(counts.at[0], counts.at[1], c=1 - core)]
    go(stage_back, 0)
    go(stage_second, 2)
    reads_part = list(here.pending)
    arrive(count_flight)
    counts[2] = counts[0] + counts[1]
    count_flight = []
    for j in range(1, 4):
        other = here.off("z", j)
        src = counts.at[2, rows_of(other * 64, 64)]
        count_flight.append(here.send(src, countz.at[j - 1], z=other))
    go(stage_back, 1)
    go(stage_wide, 0)
    go(stage_back, 2)
    arrive(count_flight)
    countz[3] = (counts[2, rows_of(z * 64, 64)] + countz[0]) + (countz[1] + countz[2])
    count_flight = []
    for j in range(1, 4):
        other = here.off("x", j)
        count_flight.append(here.send(countz.at[3, rows_of(other * 16, 16)], countx.at[j - 1], x=other))
    go(stage_wide, 1)
    go(stage_wide, 2)
    go(stage_last, 0)
    go(stage_last, 1)
    arrive(count_flight)
    countx[3] = (countz[3, rows_of(xx * 16, 16)] + countx[0]) + (countx[1] + countx[2])
    count_flight = []
    for j in range(1, 4):
        count_flight.append(here.send(countx.at[3], county.at[j - 1], y=here.off("y", j)))
    for t in GROUPS[0] + GROUPS[1]:
        arrive(flight[t])

    def load(cols):
        def one(i, carry):
            band = rows_of(i * 64, 64)
            ah[band, cols], al[band, cols] = split(full[rows_of((i * 64 + core * 512) % D, 64), cols])
            return carry

        lax.fori_loop(0, D // 64, one, 0)

    load(slice(0, SPLIT))
    here.drain(reads_part)
    go(stage_last, 2)
    for i, band, cols in tiles(0, 1, 2, 3):
        part[band, cols] = tile(i, band, cols, ah, al, slice(0, SPLIT))
    for t in GROUPS[2]:
        arrive(flight[t])
    load(slice(SPLIT, D))
    trace, square = jnp.zeros((1, 1), F32), jnp.zeros((1, 1), F32)
    for i, band, cols in tiles(0, 1, 2, 3):
        value = tile(i, band, cols, ah, al, slice(SPLIT, D)) + part[band, cols]
        if band == cols:
            trace += total_of(jnp.where(diagonal(), value, 0.0))
            square += total_of(value * value)
        else:
            square += 2.0 * total_of(value * value)
        part[band, cols] = value
        store_split(gh, gl, band, cols, value)

    norm = 1.0 / (trace + 1e-06)
    scale = jnp.sqrt(jnp.sqrt(square * norm * norm + 1e-06))
    unit = norm / (scale * scale)
    front = jnp.sqrt(norm) / scale

    def polynomial(front, unit):
        cb, cc = B * front * unit, C * front * unit
        for i, band, cols in tiles(0, 1, 2, 3):
            value = cb * part[band, cols] + cc * (unit * tile(i, band, cols, gh, gl))
            if band == cols:
                value = value + jnp.where(diagonal(), A * front, 0.0)
            store_split(qh, ql, band, cols, value)

    def product(band, h, l):
        return dot(qh[band, :], h[...]) + (dot(qh[band, :], l[...]) + dot(ql[band, :], h[...]))

    polynomial(front, unit)

    halves = []
    for i in range(2):
        band, there = slice(i * STEP, (i + 1) * STEP), slice(512 + i * STEP, 512 + (i + 1) * STEP)
        bh[band, :], bl[band, :] = split(product(band, ah, al))
        halves.append(here.send(bh.at[band], bh.at[there], c=1 - core))
        halves.append(here.send(bl.at[band], bl.at[there], c=1 - core))

    def gram(i, band, cols):
        value = tile(i, band, cols, bh, bl)
        part[band, cols] = value
        store_split(gh, gl, band, cols, value)

    low, high, right = slice(0, STEP), slice(STEP, 512), slice(512, D)
    gram(0, low, low)
    gram(0, low, high)
    gram(1, high, high)
    arrive(halves)
    gram(0, low, right)
    gram(1, high, right)
    for i, band, cols in tiles(2, 3):
        gram(i, band, cols)
    one = jnp.ones((1, 1), F32)
    polynomial(one, one)

    turned = {}

    def turn(pair_of_bands):
        to = here.off("y", 2 * pair_of_bands + core + 1)
        local = rows_of((to + 2 * core) % 4 * STEP, STEP)
        band = rows_of(to * STEP, STEP)
        ah[band, :] = product(local, bh, bl).astype(BF16)
        turned[pair_of_bands] = [here.send(ah.at[band], ah.at[band], c=1 - core)]

    def tally(n):
        to = here.off("y", n + 1)
        if n % 2 == 0:
            arrive(turned[n // 2])
        band = rows_of(to * STEP, STEP)
        rot = dot(x[...], ah[band, :], NT).astype(BF16)
        rot_ref[:, band] = rot
        for p in range(2):
            m = (to * 2 + p) * 8
            res = dot(hot[pl.ds(m, 8)].reshape(8 * CODES, rows), rot[:, p * LANES : (p + 1) * LANES])
            sums = res[:CODES]
            for mm in range(1, 8):
                sums = jnp.where(lane // SUBDIM == mm, res[mm * CODES : (mm + 1) * CODES], sums)
            slab[n, p] = sums
        swap[n] = [here.send(slab.at[n, 1 - core], pair.at[n], c=1 - core)]

    def spray(n):
        to = here.off("y", n + 1)
        arrive(swap[n])
        pair[n] += slab[n, core]
        for k in range(16):
            i, j = here.off("z", k // 4), here.off("x", k % 4)
            block = rows_of((i * 4 + j) * 16, 16)
            if n == 3 and k == 0:
                sums_in[n * 16 + k] = pair[n, block]
            else:
                landed.append(here.send(pair.at[n, block], sums_in.at[n * 16 + k], z=i, x=j, y=to))

    swap, landed = {}, []
    turn(0)
    turn(1)
    tally(0)
    tally(1)
    spray(0)
    tally(2)
    spray(1)
    tally(3)
    spray(2)
    spray(3)

    arrive(count_flight)
    count = (countx[3] + county[0]) + (county[1] + county[2])
    row = lax.broadcasted_iota(jnp.int32, (LANES, LANES), 0)
    col = lax.broadcasted_iota(jnp.int32, (LANES, LANES), 1)
    spread = jnp.where(row == (y * 2 + core) * 8 + col // SUBDIM, 1.0, 0.0)
    count = jnp.dot(count, spread, precision=lax.Precision.HIGHEST, preferred_element_type=F32)

    sums = jnp.zeros((16, LANES), F32)
    arrive(landed)
    for n in range(64):
        sums = sums + sums_in[n]
    mean_ref[...] = (sums / count).T
    here.drain()


def per_device(residuals, codes, codebook):
    rows = residuals.shape[0]
    anywhere = pl.BlockSpec(memory_space=pltpu.HBM)
    vmem = pltpu.VMEM
    matrix = [vmem((D, D), BF16)]
    rotated, mean = pl.pallas_call(
        kernel,
        out_shape=(
            jax.ShapeDtypeStruct((rows, D), BF16),
            jax.ShapeDtypeStruct((LANES, 16), F32),
        ),
        in_specs=[anywhere] * 3,
        out_specs=[pl.BlockSpec(memory_space=pltpu.VMEM)] * 2,
        scratch_shapes=[
            vmem((SUBS, rows), jnp.int32),
            vmem((SUBS, SUBDIM, CODES), BF16),
            vmem((rows, D), BF16),
            vmem((SUBS, CODES, rows), BF16),
            vmem((D, rows), BF16),
            vmem((D, D), F32),
            vmem((D, D), F32),
            vmem((512, D), F32),
            vmem((3, 128, D), F32),
            vmem((15, 8, D), F32),
        ]
        + matrix * 8
        + [
            vmem((4, 2, CODES, LANES), F32),
            vmem((4, CODES, LANES), F32),
            vmem((64, 16, LANES), F32),
            vmem((3, CODES, LANES), F32),
            vmem((4, 64, LANES), F32),
            vmem((4, 16, LANES), F32),
            vmem((3, 16, LANES), F32),
            pltpu.SemaphoreType.DMA((3,)),
            pltpu.SemaphoreType.DMA((400,)),
            pltpu.SemaphoreType.DMA((400,)),
        ],
        compiler_params=pltpu.CompilerParams(
            collective_id=0, has_side_effects=True, vmem_limit_bytes=52 * 2**20
        ),
    )(*(pltpu.with_memory_space_constraint(a, pltpu.HBM) for a in (codes.T, codebook, residuals)))
    return rotated, mean.reshape(8, SUBDIM, 16)


def solution(mesh):
    return jax.shard_map(
        per_device,
        mesh=mesh,
        in_specs=(P(("rows", "sub"), None), P(("rows", "sub"), None), P()),
        out_specs=(P(("rows", "sub"), None), P("sub", None, "rows")),
        check_vma=False,
    )
```
